32 devices in a mesh: groups: 2 (over y), chan: 4 (over z), tm: 2 (over x), beam: 2 (over core).
Axes of the slice: x: 2, y: 2, z: 4, core: 2. Of those that a mesh axis runs over, the one named last changes fastest.
Arguments:
- voltages: bfloat16 [1024, 32768], P(('groups', 'chan', 'beam'), 'tm'), parts along dimension 0, may hold values from -6 to 6
- filter_taps: float32 [8, 1024], replicated, may hold values from -0.09375 to 0.09375
- beam_weights: bfloat16 [256, 2, 1024], replicated, may hold values from -0.25 to 0.25
- station_index: int32 [512], replicated, may hold values from 0 to 255, as said below
- delay_table: int32 [512, 8], P('chan'), may hold values from 0 to 32, as said below
Outputs:
- dedispersed: float32 [2048, 8, 32], P(('groups', 'chan', 'beam'), None, 'tm'), parts along dimension 0
The draws below stay inside these ranges and needn't reach their ends.
There are 2 independent parts, one for each index of `groups`. The reference program is written for one: setup_inputs(seed, part) draws one part's arguments, and reference() takes and returns one part's arrays. A program takes and returns all parts, laid end to end along the dimension named above; an argument that names none is the same for every part. Nothing has to cross between parts.
Inputs may be any that keep to these rules, and one draw needn't show every extreme that they name: `station_index`: the even inputs name each of the 256 weight rows once, and so do the odd inputs. `delay_table`: some entry equals 32.
All inputs are finite; a program needn't handle non-finite values.
Results may differ from the reference program's by a relative error of at most 0.0029.
Values may be sent and summed in bfloat16 or wider, within the bound.
No kernel may reach another device: no remote copies, remote signals or barrier semaphores. Data moves between devices by JAX's collectives and lax.ppermute only.
A program may use at most 64 MiB of HBM per device.

```python
import math
import jax
import jax.numpy as jnp
from jax import lax

INPUTS = 512
STATIONS = 256
NFFT = 1024
CHANNELS = 512
TAPS = 8
BEAMS = 1024
NDM = 8
MAXD = 32
FRAMES = 32
SAMPLES = 32768


def draw_station_index(key, part):
    even_order = jax.random.permutation(jax.random.fold_in(key, 11), STATIONS).astype(jnp.int32)
    odd_order = jax.random.permutation(jax.random.fold_in(key, 12), STATIONS).astype(jnp.int32)
    return jnp.stack([even_order, odd_order], axis=1).reshape(INPUTS).astype(jnp.int32)


def draw_delay_table(key, part):
    table = jax.random.randint(jax.random.fold_in(key, 21), (CHANNELS, NDM), 0, MAXD + 1, dtype=jnp.int32)
    marked_row = jax.random.randint(jax.random.fold_in(key, 22), (), 0, CHANNELS, dtype=jnp.int32)
    marked_col = jax.random.randint(jax.random.fold_in(key, 23), (), 0, NDM, dtype=jnp.int32)
    row_match = jnp.arange(CHANNELS, dtype=jnp.int32)[:, None] == marked_row
    col_match = jnp.arange(NDM, dtype=jnp.int32)[None, :] == marked_col
    return jnp.where(row_match & col_match, MAXD, table).astype(jnp.int32)


def block_levels(stream_key, shape, split, low, largest):
    gain, own = 1.0, jax.random.fold_in(stream_key, 6)
    for axis_at, blocks in split:
        draws = jnp.exp(jax.random.uniform(jax.random.fold_in(own, axis_at), (blocks,), jnp.float32, low / len(split), largest / len(split)))
        gain = gain * jnp.repeat(draws, shape[axis_at] // blocks).reshape([-1 if axis == axis_at else 1 for axis in range(len(shape))])
    return gain


def bell_draw(key, dims, spread, bound, split=(), held_as=jnp.bfloat16):
    drawn = spread * jax.random.normal(key, dims, jnp.float32)
    if split:
        drawn = drawn * block_levels(key, dims, split, -0.22, 0.18)
    return jnp.clip(drawn, -bound, bound).astype(held_as)


def setup_inputs(seed: int = 0, part: int = 0) -> dict:
    keys = jax.random.split(jax.random.key(seed), 6)
    part_keys = jax.random.split(jax.random.fold_in(keys[5], part), 6)
    return {
        "voltages": bell_draw(part_keys[0], (INPUTS, SAMPLES), 1.0, 6.0, ((0, 8), (1, 2))),
        "filter_taps": bell_draw(keys[1], (TAPS, NFFT), (NFFT * TAPS // 2) ** -0.5, 0.09375, (), jnp.float32),
        "beam_weights": bell_draw(keys[2], (STATIONS, 2, BEAMS), INPUTS ** -0.5, 0.25),
        "station_index": draw_station_index(jax.random.fold_in(keys[5], 71), part),
        "delay_table": draw_delay_table(jax.random.fold_in(keys[5], 71), part),
    }


def dft_table(length):
    sample = jnp.arange(length, dtype=jnp.int32)
    column = jnp.arange(length // 2, dtype=jnp.int32)
    phase_index = sample[:, None] * column[None, :] % length
    angle_rad = phase_index.astype(jnp.float32) * (2.0 * math.pi / length)
    return jnp.stack([jnp.cos(angle_rad), -jnp.sin(angle_rad)], axis=1).astype(jnp.bfloat16)

def make_mixer(station_rows):
    real_part = station_rows[:, 0, :]
    imag_part = station_rows[:, 1, :]
    upper = jnp.concatenate([real_part, imag_part], axis=1)
    lower_half = jnp.concatenate([-imag_part, real_part], axis=1)
    return jnp.concatenate([upper, lower_half], axis=0)

def reference(voltages, filter_taps, beam_weights, station_index, delay_table):
    leading = jnp.zeros((INPUTS, (TAPS - 1) * NFFT), jnp.bfloat16)
    extended = jnp.concatenate([leading, voltages], axis=1).reshape(INPUTS, FRAMES + TAPS - 1, NFFT)
    filtered = jnp.zeros((INPUTS, FRAMES, NFFT), jnp.float32)
    for t in range(TAPS):
        filtered = filtered + filter_taps[t] * extended[:, t:t + FRAMES].astype(jnp.float32)
    filtered = filtered.astype(jnp.bfloat16)
    spectra = jnp.dot(filtered.reshape(INPUTS * FRAMES, NFFT), dft_table(NFFT).reshape(NFFT, NFFT), preferred_element_type=jnp.float32).astype(jnp.bfloat16)
    spectra = spectra.reshape(STATIONS, 2, FRAMES, 2, CHANNELS)
    pairs = station_index.reshape(STATIONS, 2)
    stacks = []
    mixers = []
    for p in range(2):
        stacks.append(jnp.transpose(spectra[:, p], (3, 1, 2, 0)).reshape(CHANNELS, FRAMES, 2 * STATIONS))
        mixers.append(make_mixer(beam_weights[pairs[:, p]]))

    def channel_power(pair_stacks):
        power_grid = jnp.zeros((FRAMES, BEAMS), jnp.float32)
        for p in range(2):
            voltage = jnp.dot(pair_stacks[p], mixers[p], preferred_element_type=jnp.float32)
            real_part = voltage[:, :BEAMS]
            imag_part = voltage[:, BEAMS:]
            power_grid = power_grid + real_part * real_part + imag_part * imag_part
        return power_grid
    power_grid = lax.map(channel_power, (stacks[0], stacks[1]))
    baseline = lax.optimization_barrier(jnp.sum(power_grid, axis=1)) / FRAMES
    excess = (power_grid - baseline[:, None, :]).astype(jnp.bfloat16)
    padded = jnp.pad(excess, ((0, 0), (0, MAXD), (0, 0)))
    channel_rows = jnp.arange(CHANNELS, dtype=jnp.int32)[:, None]
    offsets = jnp.arange(FRAMES, dtype=jnp.int32)[None, :]
    curves = []
    for d in range(NDM):
        picked = padded[channel_rows, delay_table[:, d][:, None] + offsets, :]
        curves.append(lax.optimization_barrier(jnp.sum(picked, axis=0, dtype=jnp.float32)))
    stacked_curves = jnp.transpose(jnp.stack(curves, axis=0), (2, 0, 1))
    return stacked_curves * (1.0 / math.sqrt(CHANNELS))
```

```python
import functools
import math

import jax
import jax.numpy as jnp
import numpy as np
from jax import lax
from jax.experimental import pallas as pl
from jax.experimental.pallas import tpu as pltpu
from jax.sharding import PartitionSpec as P

VMEM_BYTES = 48 << 20
LANES = 128
WIDE = 256
ROW_BLOCK = 32


def rotated(value, axis, steps):
    count = lax.axis_size(axis)
    return lax.ppermute(value, axis, [(source, (source + steps) % count) for source in range(count)])


def from_previous(value, axis):
    count = lax.axis_size(axis)
    return lax.ppermute(value, axis, [(source, source + 1) for source in range(count - 1)])


def dft_blocks(length, blocks):
    channels = length // 2
    phase = (np.arange(length)[:, None] * np.arange(channels)[None, :] % length) * (2.0 * math.pi / length)
    table = np.stack([np.cos(phase), -np.sin(phase)], axis=1).reshape(length, 2, blocks, channels // blocks)
    return jnp.asarray(np.transpose(table, (2, 0, 1, 3)).reshape(blocks, length, -1), jnp.bfloat16)


def rolled(value, start, axis):
    count = value.shape[axis]
    return lax.dynamic_slice_in_dim(jnp.concatenate([value, value], axis=axis), start, count, axis)


def vmem_spec():
    return pl.BlockSpec(memory_space=pltpu.VMEM)


def spectra_kernel(first, frames, length, has_rim, *refs):
    me_ref, refs = refs[0], refs[1:]
    rim_ref, refs = (refs[0], refs[1:]) if has_rim else (None, refs)
    volt_ref, taps_ref, dft_ref = refs[:3]
    outs, (filt, spread) = refs[3:-2], refs[-2:]
    taps = taps_ref.shape[0]
    rows = volt_ref.shape[0]
    row_block = spread.shape[1]
    half = row_block // 2

    def columns(n, _):
        lane = pl.multiple_of(n * LANES, LANES)
        weights = [taps_ref[t : t + 1, pl.ds(lane, LANES)] for t in range(taps)]

        def load(row, frame):
            if frame < 0:
                ref, frame = rim_ref, frame + taps - 1
            else:
                ref = volt_ref
            at = pl.multiple_of(frame * length + lane, LANES)
            return ref[pl.ds(row, row_block), pl.ds(at, LANES)].astype(jnp.float32)

        for block in range(rows // row_block):
            row = block * row_block
            window = [load(row, first + t - (taps - 1)) for t in range(taps - 1)]
            for f in range(frames):
                window.append(load(row, first + f))
                total = weights[0] * window[0]
                for t in range(1, taps):
                    total = total + weights[t] * window[t]
                window.pop(0)
                slot = (block * frames + f) % spread.shape[0]
                spread[slot] = total
                for p in range(2):
                    picked = spread[slot, pl.ds(p, half, stride=2), :]
                    filt[pl.ds((f * 2 + p) * (rows // 2) + block * half, half), pl.ds(lane, LANES)] = picked.astype(
                        jnp.bfloat16
                    )
        return 0

    lax.fori_loop(0, length // LANES, columns, 0)
    count = dft_ref.shape[0]
    stations = rows // 2
    channels = outs[0].shape[-1]
    for d, out in enumerate(outs):
        block = lax.rem(me_ref[0] + d, count)
        result = jnp.dot(filt[...], dft_ref[block], preferred_element_type=jnp.float32).astype(jnp.bfloat16)
        for f in range(frames):
            for p in range(2):
                at = (f * 2 + p) * stations
                for r in range(2):
                    out[f, p, r] = result[at : at + stations, r * channels : (r + 1) * channels]


def make_spectra(me, rim, voltages, filter_taps, dft, first, frames):
    rows = voltages.shape[0]
    length = filter_taps.shape[1]
    count = dft.shape[0]
    channels = dft.shape[2] // 2
    has_rim = rim is not None
    operands = ([rim] if has_rim else []) + [voltages, filter_taps, dft]
    shape = (frames, 2, 2, rows // 2, channels)
    return pl.pallas_call(
        functools.partial(spectra_kernel, first, frames, length, has_rim),
        out_shape=[jax.ShapeDtypeStruct(shape, jnp.bfloat16)] * count,
        in_specs=[pl.BlockSpec(memory_space=pltpu.SMEM)] + [vmem_spec()] * len(operands),
        out_specs=[vmem_spec()] * count,
        scratch_shapes=[
            pltpu.VMEM((frames * rows, length), jnp.bfloat16),
            pltpu.VMEM((8, min(rows, ROW_BLOCK), LANES), jnp.float32),
        ],
        compiler_params=pltpu.CompilerParams(vmem_limit_bytes=VMEM_BYTES),
        cost_estimate=pl.CostEstimate(
            flops=2 * frames * rows * length * length, bytes_accessed=8 << 20, transcendentals=0
        ),
        name=f"spectra_{first}",
    )(me, *operands)


def beam_kernel(pieces, has_sum, *refs):
    spectra, refs = refs[:pieces], refs[pieces:]
    mixers_ref, place_ref, refs = refs[0], refs[1], refs[2:]
    sums, refs = (refs[0], refs[1:]) if has_sum else (None, refs)
    out, high, low = refs
    frames, _, _, stations, channels = spectra[0].shape
    beams = mixers_ref.shape[1] // 2
    step = min(frames, max(1, WIDE // channels))

    def group(i, _):
        power = None
        for p in range(2):
            sides = []
            for side in range(step):
                parts = []
                for piece in spectra:
                    for r in range(2):
                        parts.append(piece[i * step + side, p, r])
                sides.append(jnp.concatenate(parts, axis=0))
            stacked = jnp.concatenate(sides, axis=1)
            voltage = jnp.dot(mixers_ref[p], stacked, preferred_element_type=jnp.float32)
            real_part, imag_part = voltage[:beams], voltage[beams:]
            term = real_part * real_part + imag_part * imag_part
            power = term if power is None else power + term
        upper = power.astype(jnp.bfloat16)
        at = pl.multiple_of(i * step * channels, step * channels)
        high[:, pl.ds(at, step * channels)] = upper
        low[:, pl.ds(at, step * channels)] = (power - upper.astype(jnp.float32)).astype(jnp.bfloat16)
        return 0

    lax.fori_loop(0, frames // step, group, 0)
    total = jnp.dot(high[...], place_ref[...], preferred_element_type=jnp.float32)
    total = total + jnp.dot(low[...], place_ref[...], preferred_element_type=jnp.float32)
    if has_sum:
        total = total + sums[...]
    out[...] = total


def beam_sums(spectra, mixers, place, sums):
    frames, _, _, stations, channels = spectra[0].shape
    beams = mixers.shape[1] // 2
    operands = [*spectra, mixers, place] + ([] if sums is None else [sums])
    return pl.pallas_call(
        functools.partial(beam_kernel, len(spectra), sums is not None),
        out_shape=jax.ShapeDtypeStruct((beams, place.shape[1]), jnp.float32),
        in_specs=[vmem_spec()] * len(operands),
        out_specs=vmem_spec(),
        scratch_shapes=[pltpu.VMEM((beams, frames * channels), jnp.bfloat16)] * 2,
        compiler_params=pltpu.CompilerParams(vmem_limit_bytes=VMEM_BYTES),
        cost_estimate=pl.CostEstimate(
            flops=2 * 2 * frames * channels * mixers.shape[1] * mixers.shape[2],
            bytes_accessed=8 << 20,
            transcendentals=0,
        ),
        name="beam_sums_first" if sums is None else "beam_sums_rest",
    )(*operands)


def make_mixers(beam_weights, station_index, in_dev):
    chan_devices = lax.axis_size("chan")
    beam_devices = lax.axis_size("beam")
    here, core = lax.axis_index("chan"), lax.axis_index("beam")
    stations = beam_weights.shape[0]
    arranged = beam_weights.reshape(stations, 2, chan_devices, beam_devices, -1)
    chosen = lax.dynamic_index_in_dim(arranged, core, 3, keepdims=False)
    chosen = rolled(chosen, here, 2).reshape(stations, 2, -1)
    order = station_index.reshape(chan_devices, beam_devices, in_dev // 2, 2)
    order = rolled(order[::-1], chan_devices - 1 - here, 0)
    order = rolled(order, core, 1)
    order = jnp.transpose(order, (3, 0, 1, 2))
    order = jnp.broadcast_to(order[:, :, :, None, :], (*order.shape[:3], 2, in_dev // 2)).reshape(2, -1)
    imag_column = (jnp.arange(order.shape[1], dtype=jnp.int32) // (in_dev // 2) % 2 == 1)[None, None, :]
    select = (order[:, None, :] == jnp.arange(stations, dtype=jnp.int32)[None, :, None]).astype(jnp.bfloat16)
    picked = jnp.einsum("trb,ptj->prbj", chosen, select, preferred_element_type=jnp.float32)
    real_part, imag_part = picked[:, 0], picked[:, 1]
    upper = jnp.where(imag_column, -imag_part, real_part)
    lower = jnp.where(imag_column, real_part, imag_part)
    return jnp.concatenate([upper, lower], axis=1).astype(jnp.bfloat16)


def make_place(delay_table, frames_dev):
    channels, curves = delay_table.shape
    groups = lax.axis_size("tm")
    here = lax.axis_index("tm")
    total = groups * frames_dev
    target = lax.rem(here + jnp.arange(groups, dtype=jnp.int32), groups)
    wanted = target[:, None] * frames_dev + jnp.arange(frames_dev, dtype=jnp.int32)[None, :]
    source = wanted[None, :, None, :] + delay_table[:, None, :, None]
    source = source.reshape(channels, -1)
    own = here * frames_dev + jnp.arange(frames_dev, dtype=jnp.int32)
    hit = (source[None] == own[:, None, None]).astype(jnp.float32)
    base = jnp.where(source < total, 1.0 / total, 0.0)[None]
    return (hit - base).astype(jnp.bfloat16).reshape(frames_dev * channels, -1)


def shards(voltages, filter_taps, beam_weights, station_index, delay_table):
    taps, length = filter_taps.shape
    in_dev = voltages.shape[0]
    frames_dev = voltages.shape[1] // length
    chan_devices = lax.axis_size("chan")
    beam_devices = lax.axis_size("beam")
    time_devices = lax.axis_size("tm")
    channels = delay_table.shape[0]
    curves = delay_table.shape[1]
    me = lax.axis_index("chan").astype(jnp.int32).reshape(1)
    dft = dft_blocks(length, chan_devices)
    rim = from_previous(voltages[:, (frames_dev - taps + 1) * length :], "tm")
    split = frames_dev // 2
    mixers = make_mixers(beam_weights, station_index, in_dev)
    place = make_place(delay_table, frames_dev)
    sums = None
    for first in (split, 0):
        own = make_spectra(me, rim if first < taps - 1 else None, voltages, filter_taps, dft, first, split)
        pieces = []
        for d in range(chan_devices):
            here = own[d] if d == 0 else rotated(own[d], "chan", d)
            pieces.append(here)
            for e in range(1, beam_devices):
                pieces.append(rotated(here, "beam", beam_devices - e))
        sums = beam_sums(pieces, mixers, place[first * channels : (first + split) * channels], sums)
    width = curves * frames_dev
    here = sums[:, :width]
    for e in range(1, time_devices):
        here = here + rotated(sums[:, e * width : (e + 1) * width], "tm", e)
    share = here.shape[0] // chan_devices
    final = here[:share]
    for d in range(1, chan_devices):
        final = final + rotated(here[d * share : (d + 1) * share], "chan", d)
    return (final * (1.0 / math.sqrt(length // 2))).reshape(share, curves, frames_dev)


def solution(mesh):
    in_specs = (P(("groups", "chan", "beam"), "tm"), P(), P(), P(), P("chan", None))
    out_specs = P(("groups", "chan", "beam"), None, "tm")
    return jax.shard_map(shards, mesh=mesh, in_specs=in_specs, out_specs=out_specs, check_vma=False)
```

```python
import functools
import math

import jax
import jax.numpy as jnp
import numpy as np
from jax import lax
from jax.experimental import pallas as pl
from jax.experimental.pallas import tpu as pltpu
from jax.sharding import PartitionSpec as P

VMEM_BYTES = 24 << 20
ALL_VMEM_BYTES = 60 << 20
LANES = 128
SMALL_COST = 1024
WIDE = 256
ROW_BLOCK = 32


def partner(index, step, count):
    return index ^ (-step % count) if count & (count - 1) == 0 else (index + step) % count


def source_of(index, step, count):
    return index ^ (-step % count) if count & (count - 1) == 0 else (index - step) % count


def exchanged(value, axis, step):
    count = lax.axis_size(axis)
    return lax.ppermute(value, axis, [(source, partner(source, step, count)) for source in range(count)])


def picked_blocks(value, axis, indices):
    return jnp.concatenate([lax.dynamic_slice_in_dim(value, i, 1, axis) for i in indices], axis=axis)


def from_previous(value, axis):
    count = lax.axis_size(axis)
    return lax.ppermute(value, axis, [(source, source + 1) for source in range(count - 1)])


def dft_blocks(length, blocks):
    channels = length // 2
    phase = (np.arange(length)[:, None] * np.arange(channels)[None, :] % length) * (2.0 * math.pi / length)
    table = np.stack([np.cos(phase), -np.sin(phase)], axis=1).reshape(length, 2, blocks, channels // blocks)
    return jnp.asarray(np.transpose(table, (2, 0, 1, 3)).reshape(blocks, length, -1), jnp.bfloat16)


def vmem_spec():
    return pl.BlockSpec(memory_space=pltpu.VMEM)


def spectra_kernel(first, frames, length, has_rim, *refs):
    me_ref, refs = refs[0], refs[1:]
    rim_hbm, refs = (refs[0], refs[1:]) if has_rim else (None, refs)
    volt_hbm, taps_hbm, dft_hbm = refs[:3]
    outs, (volt, taps_ref, dft_ref, filt, spread, made, sems) = refs[3:-7], refs[-7:]
    taps = taps_ref.shape[0]
    rows = volt.shape[1]
    row_block = spread.shape[1]
    half = row_block // 2
    history = taps - 1

    copies = [pltpu.make_async_copy(taps_hbm, taps_ref, sems.at[0])]
    for slot in range(history + frames):
        frame = first + slot - history
        source, at = (rim_hbm, (frame + history) * length) if frame < 0 else (volt_hbm, frame * length)
        copies.append(pltpu.make_async_copy(source.at[:, pl.ds(at, length)], volt.at[slot], sems.at[2 + slot]))
    table_copy = pltpu.make_async_copy(dft_hbm, dft_ref, sems.at[1])
    for copy in copies:
        copy.start()
    table_copy.start()
    for copy in copies:
        copy.wait()

    def columns(n, _):
        lane = pl.multiple_of(n * LANES, LANES)
        weights = [taps_ref[t : t + 1, pl.ds(lane, LANES)] for t in range(taps)]
        for block in range(rows // row_block):
            row = block * row_block

            def load(slot):
                return volt[slot, row : row + row_block, pl.ds(lane, LANES)].astype(jnp.float32)

            window = [load(t) for t in range(history)]
            for f in range(frames):
                window.append(load(f + history))
                total = weights[0] * window[0]
                for t in range(1, taps):
                    total = total + weights[t] * window[t]
                window.pop(0)
                slot = (block * frames + f) % spread.shape[0]
                spread[slot] = total
                for p in range(2):
                    picked = spread[slot, pl.ds(p, half, stride=2), :]
                    filt[pl.ds((f * 2 + p) * (rows // 2) + block * half, half), pl.ds(lane, LANES)] = picked.astype(
                        jnp.bfloat16
                    )
        return 0

    lax.fori_loop(0, length // LANES, columns, 0)
    table_copy.wait()
    count = dft_ref.shape[0]
    stations = rows // 2
    channels = outs[0].shape[-1]
    writes = []
    for d in (*range(1, count), 0):
        block = partner(me_ref[0], d, count)
        result = jnp.dot(filt[...], dft_ref[block], preferred_element_type=jnp.float32).astype(jnp.bfloat16)
        for f in range(frames):
            for p in range(2):
                at = (f * 2 + p) * stations
                for r in range(2):
                    made[d, f, p, r] = result[at : at + stations, r * channels : (r + 1) * channels]
        writes.append(pltpu.make_async_copy(made.at[d], outs[d], sems.at[sems.shape[0] - 1 - d]))
        writes[-1].start()
    for write in writes:
        write.wait()


def make_spectra(me, rim, voltages, filter_taps, dft, first, frames):
    rows = voltages.shape[0]
    taps, length = filter_taps.shape
    count = dft.shape[0]
    channels = dft.shape[2] // 2
    has_rim = rim is not None
    operands = ([rim] if has_rim else []) + [voltages, filter_taps, dft]
    shape = (frames, 2, 2, rows // 2, channels)
    slots = frames + taps - 1
    return pl.pallas_call(
        functools.partial(spectra_kernel, first, frames, length, has_rim),
        out_shape=[jax.ShapeDtypeStruct(shape, jnp.bfloat16)] * count,
        in_specs=[pl.BlockSpec(memory_space=pltpu.SMEM)] + [pl.BlockSpec(memory_space=pl.ANY)] * len(operands),
        out_specs=[pl.BlockSpec(memory_space=pl.ANY)] * count,
        scratch_shapes=[
            pltpu.VMEM((slots, rows, length), jnp.bfloat16),
            pltpu.VMEM((taps, length), jnp.float32),
            pltpu.VMEM(dft.shape, jnp.bfloat16),
            pltpu.VMEM((frames * rows, length), jnp.bfloat16),
            pltpu.VMEM((8, min(rows, ROW_BLOCK), LANES), jnp.float32),
            pltpu.VMEM((count, *shape), jnp.bfloat16),
            pltpu.SemaphoreType.DMA((slots + 2 + count,)),
        ],
        compiler_params=pltpu.CompilerParams(vmem_limit_bytes=ALL_VMEM_BYTES),
        cost_estimate=pl.CostEstimate(flops=SMALL_COST, bytes_accessed=SMALL_COST, transcendentals=0),
        name=f"spectra_{first}",
    )(me, *operands)


def channel_power(spectra, mixers_ref, high, low):
    frames, _, _, _, channels = spectra[0].shape
    beams = mixers_ref.shape[1] // 2
    step = min(frames, max(1, WIDE // channels))

    def group(i, over_frames):
        power = None
        for p in range(2):
            sides = []
            for side in range(step):
                parts = []
                for piece in spectra:
                    for r in range(2):
                        parts.append(piece[i * step + side, p, r])
                sides.append(jnp.concatenate(parts, axis=0))
            stacked = jnp.concatenate(sides, axis=1)
            voltage = jnp.dot(mixers_ref[p], stacked, preferred_element_type=jnp.float32)
            real_part, imag_part = voltage[:beams], voltage[beams:]
            term = real_part * real_part + imag_part * imag_part
            power = term if power is None else power + term
        upper = power.astype(jnp.bfloat16)
        at = pl.multiple_of(i * step * channels, step * channels)
        high[:, pl.ds(at, step * channels)] = upper
        low[:, pl.ds(at, step * channels)] = (power - upper.astype(jnp.float32)).astype(jnp.bfloat16)
        for side in range(step):
            over_frames = over_frames + power[:, side * channels : (side + 1) * channels]
        return over_frames

    return lax.fori_loop(0, frames // step, group, jnp.zeros((beams, channels), jnp.float32))


def placed(high, low, place_ref):
    total = jnp.dot(high[...], place_ref[...], preferred_element_type=jnp.float32)
    return total + jnp.dot(low[...], place_ref[...], preferred_element_type=jnp.float32)


def first_kernel(pieces, *refs):
    spectra, (mixers_ref, place_ref, sums_ref, level_ref, high, low) = refs[:pieces], refs[pieces:]
    level_ref[...] = channel_power(spectra, mixers_ref, high, low).astype(jnp.bfloat16)
    sums_ref[...] = placed(high, low, place_ref)


def last_kernel(pieces, levels, level_scale, *refs):
    spectra, refs = refs[:pieces], refs[pieces:]
    level_refs, refs = refs[:levels], refs[levels:]
    mixers_ref, place_ref, centre_ref, earlier_ref, out, high, low = refs
    channel_power(spectra, mixers_ref, high, low)
    level = level_refs[0][...].astype(jnp.float32)
    for ref in level_refs[1:]:
        level = level + ref[...].astype(jnp.float32)
    level = (level * level_scale).astype(jnp.bfloat16)
    total = earlier_ref[...] - jnp.dot(level, centre_ref[...], preferred_element_type=jnp.float32)
    total = total + placed(high, low, place_ref)
    blocks, share, width = out.shape
    groups = total.shape[1] // width
    for block in range(blocks):
        row, column = block // groups * share, block % groups * width
        out[block] = total[row : row + share, column : column + width].astype(jnp.bfloat16)


def beam_call(kernel, name, out_shape, spectra, mixers, *rest):
    frames, _, _, _, channels = spectra[0].shape
    beams = mixers.shape[1] // 2
    operands = [*spectra, *rest]
    return pl.pallas_call(
        kernel,
        out_shape=out_shape,
        in_specs=[vmem_spec()] * len(operands),
        out_specs=jax.tree.map(lambda _: vmem_spec(), out_shape),
        scratch_shapes=[pltpu.VMEM((beams, frames * channels), jnp.bfloat16)] * 2,
        compiler_params=pltpu.CompilerParams(vmem_limit_bytes=VMEM_BYTES),
        cost_estimate=pl.CostEstimate(flops=SMALL_COST, bytes_accessed=SMALL_COST, transcendentals=0),
        name=name,
    )(*operands)


def tables_kernel(total, *refs):
    where_ref, order_ref, weights_ref, delay_ref, mixers_ref, place_ref, centre_ref = refs
    time = where_ref[0]
    stations = weights_ref.shape[1]
    beams = mixers_ref.shape[1] // 2
    inputs = mixers_ref.shape[2]
    station = lax.broadcasted_iota(jnp.int32, (stations, inputs), 0)
    imag_column = order_ref[2:3, :] == 1
    for p in range(2):
        select = (station == order_ref[p : p + 1, :]).astype(jnp.bfloat16)
        picked = []
        for r in range(2):
            picked.append(
                lax.dot_general(
                    weights_ref[r], select, (((0,), (0,)), ((), ())), preferred_element_type=jnp.float32
                )
            )
        real_part, imag_part = picked
        mixers_ref[p, :beams, :] = jnp.where(imag_column, -imag_part, real_part).astype(jnp.bfloat16)
        mixers_ref[p, beams:, :] = jnp.where(imag_column, real_part, imag_part).astype(jnp.bfloat16)
    channels, curves = delay_ref.shape
    frames, _, width = place_ref.shape
    lane = lax.broadcasted_iota(jnp.int32, (1, width), 1)
    curve = lane // frames % curves
    wanted = lane // (frames * curves) * frames + lane % frames
    source = jnp.broadcast_to(wanted, (channels, width))
    for d in range(curves):
        source = source + jnp.where(curve == d, delay_ref[:, d : d + 1], 0)
    base = jnp.where(source < total, 1.0 / total, 0.0)
    for f in range(frames):
        hit = jnp.where(source == time * frames + f, 1.0, 0.0)
        place_ref[f] = (hit - base).astype(jnp.bfloat16)
    held = jnp.where((source >= time * frames) & (source < (time + 1) * frames), 1.0, 0.0)
    centre_ref[...] = (held - base * frames).astype(jnp.bfloat16)


def make_tables(beam_weights, station_index, delay_table, in_dev, frames_dev):
    chan_devices = lax.axis_size("chan")
    beam_devices = lax.axis_size("beam")
    time_devices = lax.axis_size("tm")
    here, core = lax.axis_index("chan"), lax.axis_index("beam")
    stations = beam_weights.shape[0]
    arranged = jnp.transpose(beam_weights, (1, 0, 2)).reshape(2, stations, chan_devices, beam_devices, -1)
    chosen = lax.dynamic_index_in_dim(arranged, core, 3, keepdims=False)
    chosen = chosen.reshape(2, stations, -1)
    order = station_index.reshape(chan_devices, beam_devices, in_dev // 2, 2)
    order = picked_blocks(order, 0, [source_of(here, d, chan_devices) for d in range(chan_devices)])
    order = picked_blocks(order, 1, [source_of(core, e, beam_devices) for e in range(beam_devices)])
    order = jnp.transpose(order, (3, 0, 1, 2))
    order = jnp.broadcast_to(order[:, :, :, None, :], (*order.shape[:3], 2, in_dev // 2)).reshape(2, -1)
    imag_column = jnp.arange(order.shape[1], dtype=jnp.int32) // (in_dev // 2) % 2
    order = jnp.concatenate([order, imag_column[None]], axis=0)
    where = lax.axis_index("tm").astype(jnp.int32).reshape(1)
    channels, curves = delay_table.shape
    beams = chosen.shape[2]
    inputs = order.shape[1]
    width = time_devices * curves * frames_dev
    return pl.pallas_call(
        functools.partial(tables_kernel, time_devices * frames_dev),
        out_shape=[
            jax.ShapeDtypeStruct((2, 2 * beams, inputs), jnp.bfloat16),
            jax.ShapeDtypeStruct((frames_dev, channels, width), jnp.bfloat16),
            jax.ShapeDtypeStruct((channels, width), jnp.bfloat16),
        ],
        in_specs=[pl.BlockSpec(memory_space=pltpu.SMEM)] + [vmem_spec()] * 3,
        out_specs=[vmem_spec()] * 3,
        compiler_params=pltpu.CompilerParams(vmem_limit_bytes=VMEM_BYTES),
        cost_estimate=pl.CostEstimate(flops=SMALL_COST, bytes_accessed=SMALL_COST, transcendentals=0),
        name="tables",
    )(where, order, chosen, delay_table)


def shards(voltages, filter_taps, beam_weights, station_index, delay_table):
    taps, length = filter_taps.shape
    in_dev = voltages.shape[0]
    frames_dev = voltages.shape[1] // length
    chan_devices = lax.axis_size("chan")
    beam_devices = lax.axis_size("beam")
    time_devices = lax.axis_size("tm")
    channels = delay_table.shape[0]
    curves = delay_table.shape[1]
    me = lax.axis_index("chan").astype(jnp.int32).reshape(1)
    dft = dft_blocks(length, chan_devices)
    history = taps - 1
    rim = from_previous(voltages[:, (frames_dev - history) * length :], "tm")
    half = frames_dev // 2
    ready = []
    for first, frames in ((half, frames_dev - half), (0, half)):
        if first < history:
            rim, mixers, place, centre = lax.optimization_barrier((rim, mixers, place, centre))
        own = list(make_spectra(me, rim if first < history else None, voltages, filter_taps, dft, first, frames))
        if first >= history:
            late, own[0] = lax.optimization_barrier(((beam_weights, station_index, delay_table), own[0]))
            mixers, place, centre = make_tables(*late, in_dev, frames_dev)
            place = place.reshape(frames_dev * channels, -1)
        arrived = {d: exchanged(own[d], "chan", d) for d in range(chan_devices - 1, 0, -1)}
        ready.append([own[0]] + [arrived[d] for d in range(1, chan_devices)])
    ready[0], ready[1][0] = lax.optimization_barrier((ready[0], ready[1][0]))

    def with_hops(arrived):
        pieces = []
        for here in arrived:
            pieces += [here] + [exchanged(here, "beam", e) for e in range(1, beam_devices)]
        return pieces

    beams = mixers.shape[1] // 2
    spectra = with_hops(ready[0])
    shapes = [
        jax.ShapeDtypeStruct((beams, place.shape[1]), jnp.float32),
        jax.ShapeDtypeStruct((beams, channels), jnp.bfloat16),
    ]
    sums, level = beam_call(
        functools.partial(first_kernel, len(spectra)),
        "beam_first",
        shapes,
        spectra,
        mixers,
        mixers,
        place[half * channels :],
    )
    levels = [level] + [exchanged(level, "tm", e) for e in range(1, time_devices)]
    ready[1], sums, levels = lax.optimization_barrier((ready[1], sums, levels))
    spectra = with_hops(ready[1])
    level_scale = 1.0 / (time_devices * (frames_dev - half))
    share = beams // chan_devices
    blocks = beam_call(
        functools.partial(last_kernel, len(spectra), len(levels), level_scale),
        "beam_last",
        jax.ShapeDtypeStruct((chan_devices * time_devices, share, curves * frames_dev), jnp.bfloat16),
        spectra,
        mixers,
        *levels,
        mixers,
        place[: half * channels],
        centre,
        sums,
    )
    blocks = lax.all_to_all(blocks, ("chan", "tm"), split_axis=0, concat_axis=0, tiled=True)
    final = jnp.sum(blocks.astype(jnp.float32), axis=0)
    return (final * (1.0 / math.sqrt(length // 2))).reshape(share, curves, frames_dev)


def solution(mesh):
    in_specs = (P(("groups", "chan", "beam"), "tm"), P(), P(), P(), P("chan", None))
    out_specs = P(("groups", "chan", "beam"), None, "tm")
    return jax.shard_map(shards, mesh=mesh, in_specs=in_specs, out_specs=out_specs, check_vma=False)
```

```python
import functools
import math

import jax
import jax.numpy as jnp
import numpy as np
from jax import lax
from jax.experimental import pallas as pl
from jax.experimental.pallas import tpu as pltpu
from jax.sharding import PartitionSpec as P

VMEM_BYTES = 24 << 20
ALL_VMEM_BYTES = 60 << 20
LANES = 128
SMALL_COST = 1024
WIDE = 256
ROW_BLOCK = 32


def partner(index, step, count):
    return index ^ (-step % count) if count & (count - 1) == 0 else (index + step) % count


def source_of(index, step, count):
    return index ^ (-step % count) if count & (count - 1) == 0 else (index - step) % count


def exchanged(value, axis, step):
    count = lax.axis_size(axis)
    return lax.ppermute(value, axis, [(source, partner(source, step, count)) for source in range(count)])


def picked_blocks(value, axis, indices):
    return jnp.concatenate([lax.dynamic_slice_in_dim(value, i, 1, axis) for i in indices], axis=axis)


def from_previous(value, axis):
    count = lax.axis_size(axis)
    return lax.ppermute(value, axis, [(source, source + 1) for source in range(count - 1)])


def dft_blocks(length, blocks):
    channels = length // 2
    phase = (np.arange(length)[:, None] * np.arange(channels)[None, :] % length) * (2.0 * math.pi / length)
    table = np.stack([np.cos(phase), -np.sin(phase)], axis=1).reshape(length, 2, blocks, channels // blocks)
    return jnp.asarray(np.transpose(table, (2, 0, 1, 3)).reshape(blocks, length, -1), jnp.bfloat16)


def vmem_spec():
    return pl.BlockSpec(memory_space=pltpu.VMEM)


def spectra_kernel(first, frames, length, has_rim, emit, *refs):
    me_ref, refs = refs[0], refs[1:]
    rim_hbm, refs = (refs[0], refs[1:]) if has_rim else (None, refs)
    volt_hbm, taps_hbm, dft_hbm = refs[:3]
    outs, (volt, taps_ref, dft_ref, filt, spread, made, sems) = refs[3:-7], refs[-7:]
    taps = taps_ref.shape[0]
    rows = volt.shape[0]
    row_block = spread.shape[1]
    half = row_block // 2
    history = taps - 1

    taps_copy = pltpu.make_async_copy(taps_hbm, taps_ref, sems.at[0])
    taps_copy.start()
    early = max(0, history - first)
    sources = [(volt_hbm, max(0, first - history) * length, early * length, (history + frames - early) * length)]
    if has_rim:
        sources.append((rim_hbm, (history - early) * length, 0, early * length))
    copies = []
    for block in range(rows // row_block):
        span = pl.ds(block * row_block, row_block)
        for n, (source, start, at, size) in enumerate(sources):
            copies.append(
                pltpu.make_async_copy(
                    source.at[span, pl.ds(start, size)],
                    volt.at[span, pl.ds(at, size)],
                    sems.at[2 + block * len(sources) + n],
                )
            )
            copies[-1].start()
    table_copy = pltpu.make_async_copy(dft_hbm, dft_ref, sems.at[1])
    writes = []
    if emit:
        *outs, rim_out = outs

    def filtered_block(block):
        row = block * row_block

        def columns(n, _):
            lane = pl.multiple_of(n * LANES, LANES)
            weights = [taps_ref[t : t + 1, pl.ds(lane, LANES)] for t in range(taps)]

            def load(slot):
                at = pl.multiple_of(slot * length + lane, LANES)
                return volt[row : row + row_block, pl.ds(at, LANES)].astype(jnp.float32)

            window = [load(t) for t in range(history)]
            for f in range(frames):
                window.append(load(f + history))
                total = weights[0] * window[0]
                for t in range(1, taps):
                    total = total + weights[t] * window[t]
                window.pop(0)
                slot = f % spread.shape[0]
                spread[slot] = total
                for p in range(2):
                    picked = spread[slot, pl.ds(p, half, stride=2), :]
                    filt[pl.ds((f * 2 + p) * (rows // 2) + row // 2, half), pl.ds(lane, LANES)] = picked.astype(
                        jnp.bfloat16
                    )
            return 0

        lax.fori_loop(0, length // LANES, columns, 0)

    for block in range(rows // row_block):
        for copy in copies[block * len(sources) : (block + 1) * len(sources)]:
            copy.wait()
        if block == 0:
            taps_copy.wait()
            table_copy.start()
        filtered_block(block)
    if emit:
        writes.append(
            pltpu.make_async_copy(volt.at[:, pl.ds(frames * length, history * length)], rim_out, sems.at[2])
        )
        writes[-1].start()
    table_copy.wait()
    count = dft_ref.shape[0]
    stations = rows // 2
    channels = outs[0].shape[-1]
    for d in (*range(1, count), 0):
        block = partner(me_ref[0], d, count)
        result = jnp.dot(filt[...], dft_ref[block], preferred_element_type=jnp.float32).astype(jnp.bfloat16)
        for f in range(frames):
            for p in range(2):
                at = (f * 2 + p) * stations
                for r in range(2):
                    made[d, f, p, r] = result[at : at + stations, r * channels : (r + 1) * channels]
        writes.append(pltpu.make_async_copy(made.at[d], outs[d], sems.at[sems.shape[0] - 1 - d]))
        writes[-1].start()
    for write in writes:
        write.wait()


def make_spectra(me, rim, voltages, filter_taps, dft, first, frames, emit):
    rows = voltages.shape[0]
    taps, length = filter_taps.shape
    count = dft.shape[0]
    channels = dft.shape[2] // 2
    has_rim = rim is not None
    operands = ([rim] if has_rim else []) + [voltages, filter_taps, dft]
    shape = (frames, 2, 2, rows // 2, channels)
    slots = frames + taps - 1
    return pl.pallas_call(
        functools.partial(spectra_kernel, first, frames, length, has_rim, emit),
        out_shape=[jax.ShapeDtypeStruct(shape, jnp.bfloat16)] * count
        + [jax.ShapeDtypeStruct((rows, (taps - 1) * length), jnp.bfloat16)] * emit,
        in_specs=[pl.BlockSpec(memory_space=pltpu.SMEM)] + [pl.BlockSpec(memory_space=pl.ANY)] * len(operands),
        out_specs=[pl.BlockSpec(memory_space=pl.ANY)] * (count + emit),
        scratch_shapes=[
            pltpu.VMEM((rows, slots * length), jnp.bfloat16),
            pltpu.VMEM((taps, length), jnp.float32),
            pltpu.VMEM(dft.shape, jnp.bfloat16),
            pltpu.VMEM((frames * rows, length), jnp.bfloat16),
            pltpu.VMEM((8, min(rows, ROW_BLOCK), LANES), jnp.float32),
            pltpu.VMEM((count, *shape), jnp.bfloat16),
            pltpu.SemaphoreType.DMA((2 * -(-rows // ROW_BLOCK) + 2 + count,)),
        ],
        compiler_params=pltpu.CompilerParams(vmem_limit_bytes=ALL_VMEM_BYTES),
        cost_estimate=pl.CostEstimate(flops=SMALL_COST, bytes_accessed=SMALL_COST, transcendentals=0),
        name=f"spectra_{first}",
    )(me, *operands)


def channel_power(spectra, mixers_ref, high, low):
    frames, _, _, _, channels = spectra[0].shape
    beams = mixers_ref.shape[1] // 2
    step = min(frames, max(1, WIDE // channels))

    def group(first, count, over_frames):
        power = None
        for p in range(2):
            sides = []
            for side in range(count):
                parts = []
                for piece in spectra:
                    for r in range(2):
                        parts.append(piece[first + side, p, r])
                sides.append(jnp.concatenate(parts, axis=0))
            stacked = jnp.concatenate(sides, axis=1)
            voltage = jnp.dot(mixers_ref[p], stacked, preferred_element_type=jnp.float32)
            real_part, imag_part = voltage[:beams], voltage[beams:]
            term = real_part * real_part + imag_part * imag_part
            power = term if power is None else power + term
        upper = power.astype(jnp.bfloat16)
        at = first * channels if isinstance(first, int) else pl.multiple_of(first * channels, step * channels)
        high[:, pl.ds(at, count * channels)] = upper
        low[:, pl.ds(at, count * channels)] = (power - upper.astype(jnp.float32)).astype(jnp.bfloat16)
        for side in range(count):
            over_frames = over_frames + power[:, side * channels : (side + 1) * channels]
        return over_frames

    whole = frames // step
    over_frames = jnp.zeros((beams, channels), jnp.float32)
    over_frames = lax.fori_loop(0, whole, lambda i, carry: group(i * step, step, carry), over_frames)
    if frames > whole * step:
        over_frames = group(whole * step, frames - whole * step, over_frames)
    return over_frames


def placed(high, low, place_ref):
    total = jnp.dot(high[...], place_ref[...], preferred_element_type=jnp.float32)
    return total + jnp.dot(low[...], place_ref[...], preferred_element_type=jnp.float32)


def first_kernel(pieces, *refs):
    spectra, (mixers_ref, place_ref, sums_ref, level_ref, high, low) = refs[:pieces], refs[pieces:]
    level_ref[...] = channel_power(spectra, mixers_ref, high, low).astype(jnp.bfloat16)
    sums_ref[...] = placed(high, low, place_ref)


def last_kernel(pieces, levels, level_scale, *refs):
    spectra, refs = refs[:pieces], refs[pieces:]
    level_refs, refs = refs[:levels], refs[levels:]
    mixers_ref, place_ref, centre_ref, earlier_ref, out, high, low = refs
    channel_power(spectra, mixers_ref, high, low)
    level = level_refs[0][...].astype(jnp.float32)
    for ref in level_refs[1:]:
        level = level + ref[...].astype(jnp.float32)
    level = (level * level_scale).astype(jnp.bfloat16)
    total = earlier_ref[...] - jnp.dot(level, centre_ref[...], preferred_element_type=jnp.float32)
    total = total + placed(high, low, place_ref)
    blocks, share, width = out.shape
    groups = total.shape[1] // width
    for block in range(blocks):
        row, column = block // groups * share, block % groups * width
        out[block] = total[row : row + share, column : column + width].astype(jnp.bfloat16)


def beam_call(kernel, name, out_shape, spectra, mixers, *rest):
    frames, _, _, _, channels = spectra[0].shape
    beams = mixers.shape[1] // 2
    operands = [*spectra, *rest]
    return pl.pallas_call(
        kernel,
        out_shape=out_shape,
        in_specs=[vmem_spec()] * len(operands),
        out_specs=jax.tree.map(lambda _: vmem_spec(), out_shape),
        scratch_shapes=[pltpu.VMEM((beams, frames * channels), jnp.bfloat16)] * 2,
        compiler_params=pltpu.CompilerParams(vmem_limit_bytes=VMEM_BYTES),
        cost_estimate=pl.CostEstimate(flops=SMALL_COST, bytes_accessed=SMALL_COST, transcendentals=0),
        name=name,
    )(*operands)


def tables_kernel(total, *refs):
    where_ref, order_ref, weights_ref, delay_ref, mixers_ref, place_ref, centre_ref = refs
    time = where_ref[0]
    stations = weights_ref.shape[1]
    beams = mixers_ref.shape[1] // 2
    inputs = mixers_ref.shape[2]
    station = lax.broadcasted_iota(jnp.int32, (stations, inputs), 0)
    imag_column = order_ref[2:3, :] == 1
    for p in range(2):
        select = (station == order_ref[p : p + 1, :]).astype(jnp.bfloat16)
        picked = []
        for r in range(2):
            picked.append(
                lax.dot_general(
                    weights_ref[r], select, (((0,), (0,)), ((), ())), preferred_element_type=jnp.float32
                )
            )
        real_part, imag_part = picked
        mixers_ref[p, :beams, :] = jnp.where(imag_column, -imag_part, real_part).astype(jnp.bfloat16)
        mixers_ref[p, beams:, :] = jnp.where(imag_column, real_part, imag_part).astype(jnp.bfloat16)
    channels, curves = delay_ref.shape
    frames, _, width = place_ref.shape
    lane = lax.broadcasted_iota(jnp.int32, (1, width), 1)
    curve = lane // frames % curves
    wanted = lane // (frames * curves) * frames + lane % frames
    source = jnp.broadcast_to(wanted, (channels, width))
    for d in range(curves):
        source = source + jnp.where(curve == d, delay_ref[:, d : d + 1], 0)
    base = jnp.where(source < total, 1.0 / total, 0.0)
    for f in range(frames):
        hit = jnp.where(source == time * frames + f, 1.0, 0.0)
        place_ref[f] = (hit - base).astype(jnp.bfloat16)
    held = jnp.where((source >= time * frames) & (source < (time + 1) * frames), 1.0, 0.0)
    centre_ref[...] = (held - base * frames).astype(jnp.bfloat16)


def make_tables(beam_weights, station_index, delay_table, in_dev, frames_dev):
    chan_devices = lax.axis_size("chan")
    beam_devices = lax.axis_size("beam")
    time_devices = lax.axis_size("tm")
    here, core = lax.axis_index("chan"), lax.axis_index("beam")
    stations = beam_weights.shape[0]
    arranged = jnp.transpose(beam_weights, (1, 0, 2)).reshape(2, stations, chan_devices, beam_devices, -1)
    chosen = lax.dynamic_index_in_dim(arranged, core, 3, keepdims=False)
    chosen = chosen.reshape(2, stations, -1)
    order = station_index.reshape(chan_devices, beam_devices, in_dev // 2, 2)
    order = picked_blocks(order, 0, [source_of(here, d, chan_devices) for d in range(chan_devices)])
    order = picked_blocks(order, 1, [source_of(core, e, beam_devices) for e in range(beam_devices)])
    order = jnp.transpose(order, (3, 0, 1, 2))
    order = jnp.broadcast_to(order[:, :, :, None, :], (*order.shape[:3], 2, in_dev // 2)).reshape(2, -1)
    imag_column = jnp.arange(order.shape[1], dtype=jnp.int32) // (in_dev // 2) % 2
    order = jnp.concatenate([order, imag_column[None]], axis=0)
    where = lax.axis_index("tm").astype(jnp.int32).reshape(1)
    channels, curves = delay_table.shape
    beams = chosen.shape[2]
    inputs = order.shape[1]
    width = time_devices * curves * frames_dev
    return pl.pallas_call(
        functools.partial(tables_kernel, time_devices * frames_dev),
        out_shape=[
            jax.ShapeDtypeStruct((2, 2 * beams, inputs), jnp.bfloat16),
            jax.ShapeDtypeStruct((frames_dev, channels, width), jnp.bfloat16),
            jax.ShapeDtypeStruct((channels, width), jnp.bfloat16),
        ],
        in_specs=[pl.BlockSpec(memory_space=pltpu.SMEM)] + [vmem_spec()] * 3,
        out_specs=[vmem_spec()] * 3,
        compiler_params=pltpu.CompilerParams(vmem_limit_bytes=VMEM_BYTES),
        cost_estimate=pl.CostEstimate(flops=SMALL_COST, bytes_accessed=SMALL_COST, transcendentals=0),
        name="tables",
    )(where, order, chosen, delay_table)


def shards(voltages, filter_taps, beam_weights, station_index, delay_table):
    taps, length = filter_taps.shape
    in_dev = voltages.shape[0]
    frames_dev = voltages.shape[1] // length
    chan_devices = lax.axis_size("chan")
    beam_devices = lax.axis_size("beam")
    time_devices = lax.axis_size("tm")
    channels = delay_table.shape[0]
    curves = delay_table.shape[1]
    me = lax.axis_index("chan").astype(jnp.int32).reshape(1)
    dft = dft_blocks(length, chan_devices)
    history = taps - 1
    half = min(taps - 1, frames_dev // 2)
    rim = None
    ready = []
    for first, frames in ((half, frames_dev - half), (0, half)):
        emit = rim is None
        if not emit:
            rim, mixers, place, centre = lax.optimization_barrier((rim, mixers, place, centre))
        own = make_spectra(me, rim, voltages, filter_taps, dft, first, frames, emit)
        if emit:
            *own, rim = own
            rim = from_previous(rim, "tm")
            late, own[0] = lax.optimization_barrier(((beam_weights, station_index, delay_table), own[0]))
            mixers, place, centre = make_tables(*late, in_dev, frames_dev)
            place = place.reshape(frames_dev * channels, -1)
        ready.append([own[0]] + [exchanged(own[d], "chan", d) for d in range(1, chan_devices)])
    ready[0], ready[1][0] = lax.optimization_barrier((ready[0], ready[1][0]))

    def with_hops(arrived):
        pieces = []
        for here in arrived:
            pieces += [here] + [exchanged(here, "beam", e) for e in range(1, beam_devices)]
        return pieces

    beams = mixers.shape[1] // 2
    spectra = with_hops(ready[0])
    shapes = [
        jax.ShapeDtypeStruct((beams, place.shape[1]), jnp.float32),
        jax.ShapeDtypeStruct((beams, channels), jnp.bfloat16),
    ]
    sums, level = beam_call(
        functools.partial(first_kernel, len(spectra)),
        "beam_first",
        shapes,
        spectra,
        mixers,
        mixers,
        place[half * channels :],
    )
    levels = [level] + [exchanged(level, "tm", e) for e in range(1, time_devices)]
    ready[1], sums, levels = lax.optimization_barrier((ready[1], sums, levels))
    spectra = with_hops(ready[1])
    level_scale = 1.0 / (time_devices * (frames_dev - half))
    share = beams // chan_devices
    blocks = beam_call(
        functools.partial(last_kernel, len(spectra), len(levels), level_scale),
        "beam_last",
        jax.ShapeDtypeStruct((chan_devices * time_devices, share, curves * frames_dev), jnp.bfloat16),
        spectra,
        mixers,
        *levels,
        mixers,
        place[: half * channels],
        centre,
        sums,
    )
    blocks = lax.all_to_all(blocks, ("chan", "tm"), split_axis=0, concat_axis=0, tiled=True)
    final = jnp.sum(blocks.astype(jnp.float32), axis=0)
    return (final * (1.0 / math.sqrt(length // 2))).reshape(share, curves, frames_dev)


def solution(mesh):
    in_specs = (P(("groups", "chan", "beam"), "tm"), P(), P(), P(), P("chan", None))
    out_specs = P(("groups", "chan", "beam"), None, "tm")
    return jax.shard_map(shards, mesh=mesh, in_specs=in_specs, out_specs=out_specs, check_vma=False)
```

```python
import functools
import math

import jax
import jax.numpy as jnp
import numpy as np
from jax import lax
from jax.experimental import pallas as pl
from jax.experimental.pallas import tpu as pltpu
from jax.sharding import PartitionSpec as P

VMEM_BYTES = 24 << 20
ALL_VMEM_BYTES = 60 << 20
LANES = 128
SMALL_COST = 1024
WIDE = 256
ROW_BLOCK = 32


def partner(index, step, count):
    return index ^ (-step % count) if count & (count - 1) == 0 else (index + step) % count


def source_of(index, step, count):
    return index ^ (-step % count) if count & (count - 1) == 0 else (index - step) % count


def exchanged(value, axis, step):
    count = lax.axis_size(axis)
    return lax.ppermute(value, axis, [(source, partner(source, step, count)) for source in range(count)])


def picked_blocks(value, axis, indices):
    return jnp.concatenate([lax.dynamic_slice_in_dim(value, i, 1, axis) for i in indices], axis=axis)


def from_previous(value, axis):
    count = lax.axis_size(axis)
    return lax.ppermute(value, axis, [(source, source + 1) for source in range(count - 1)])


def dft_blocks(length, blocks):
    channels = length // 2
    phase = (np.arange(length)[:, None] * np.arange(channels)[None, :] % length) * (2.0 * math.pi / length)
    table = np.stack([np.cos(phase), -np.sin(phase)], axis=1).reshape(length, 2, blocks, channels // blocks)
    return jnp.asarray(np.transpose(table, (2, 0, 1, 3)).reshape(blocks, length, -1), jnp.bfloat16)


def vmem_spec():
    return pl.BlockSpec(memory_space=pltpu.VMEM)


def spectra_kernel(first, frames, length, has_rim, emit, *refs):
    me_ref, refs = refs[0], refs[1:]
    rim_hbm, refs = (refs[0], refs[1:]) if has_rim else (None, refs)
    volt_hbm, taps_hbm, dft_hbm = refs[:3]
    outs, (volt, taps_ref, dft_ref, filt, spread, made, sems) = refs[3:-7], refs[-7:]
    taps = taps_ref.shape[0]
    rows = volt.shape[0]
    row_block = spread.shape[1]
    half = row_block // 2
    history = taps - 1

    taps_copy = pltpu.make_async_copy(taps_hbm, taps_ref, sems.at[0])
    taps_copy.start()
    early = max(0, history - first)
    sources = [(volt_hbm, max(0, first - history) * length, early * length, (history + frames - early) * length)]
    if has_rim:
        sources.append((rim_hbm, (history - early) * length, 0, early * length))
    copies = []
    for block in range(rows // row_block):
        span = pl.ds(block * row_block, row_block)
        for n, (source, start, at, size) in enumerate(sources):
            copies.append(
                pltpu.make_async_copy(
                    source.at[span, pl.ds(start, size)],
                    volt.at[span, pl.ds(at, size)],
                    sems.at[2 + block * len(sources) + n],
                )
            )
            copies[-1].start()
    table_copy = pltpu.make_async_copy(dft_hbm, dft_ref, sems.at[1])
    writes = []
    if emit:
        *outs, rim_out = outs

    def filtered_block(block):
        row = block * row_block

        def columns(n, _):
            lane = pl.multiple_of(n * LANES, LANES)
            weights = [taps_ref[t : t + 1, pl.ds(lane, LANES)] for t in range(taps)]

            def load(slot):
                at = pl.multiple_of(slot * length + lane, LANES)
                return volt[row : row + row_block, pl.ds(at, LANES)].astype(jnp.float32)

            window = [load(t) for t in range(history)]
            for f in range(frames):
                window.append(load(f + history))
                total = weights[0] * window[0]
                for t in range(1, taps):
                    total = total + weights[t] * window[t]
                window.pop(0)
                slot = f % spread.shape[0]
                spread[slot] = total
                for p in range(2):
                    picked = spread[slot, pl.ds(p, half, stride=2), :]
                    filt[pl.ds((f * 2 + p) * (rows // 2) + row // 2, half), pl.ds(lane, LANES)] = picked.astype(
                        jnp.bfloat16
                    )
            return 0

        lax.fori_loop(0, length // LANES, columns, 0)

    for block in range(rows // row_block):
        for copy in copies[block * len(sources) : (block + 1) * len(sources)]:
            copy.wait()
        if block == 0:
            taps_copy.wait()
            table_copy.start()
        filtered_block(block)
    if emit:
        writes.append(
            pltpu.make_async_copy(volt.at[:, pl.ds(frames * length, history * length)], rim_out, sems.at[2])
        )
        writes[-1].start()
    table_copy.wait()
    count = dft_ref.shape[0]
    stations = rows // 2
    channels = outs[0].shape[-1]
    for d in (*range(1, count), 0):
        block = partner(me_ref[0], d, count)
        result = jnp.dot(filt[...], dft_ref[block], preferred_element_type=jnp.float32).astype(jnp.bfloat16)
        for f in range(frames):
            for p in range(2):
                at = (f * 2 + p) * stations
                for r in range(2):
                    made[d, f, p, r] = result[at : at + stations, r * channels : (r + 1) * channels]
        writes.append(pltpu.make_async_copy(made.at[d], outs[d], sems.at[sems.shape[0] - 1 - d]))
        writes[-1].start()
    for write in writes:
        write.wait()


def make_spectra(me, rim, voltages, filter_taps, dft, first, frames, emit):
    rows = voltages.shape[0]
    taps, length = filter_taps.shape
    count = dft.shape[0]
    channels = dft.shape[2] // 2
    has_rim = rim is not None
    operands = ([rim] if has_rim else []) + [voltages, filter_taps, dft]
    shape = (frames, 2, 2, rows // 2, channels)
    slots = frames + taps - 1
    return pl.pallas_call(
        functools.partial(spectra_kernel, first, frames, length, has_rim, emit),
        out_shape=[jax.ShapeDtypeStruct(shape, jnp.bfloat16)] * count
        + [jax.ShapeDtypeStruct((rows, (taps - 1) * length), jnp.bfloat16)] * emit,
        in_specs=[pl.BlockSpec(memory_space=pltpu.SMEM)] + [pl.BlockSpec(memory_space=pl.ANY)] * len(operands),
        out_specs=[pl.BlockSpec(memory_space=pl.ANY)] * (count + emit),
        scratch_shapes=[
            pltpu.VMEM((rows, slots * length), jnp.bfloat16),
            pltpu.VMEM((taps, length), jnp.float32),
            pltpu.VMEM(dft.shape, jnp.bfloat16),
            pltpu.VMEM((frames * rows, length), jnp.bfloat16),
            pltpu.VMEM((8, min(rows, ROW_BLOCK), LANES), jnp.float32),
            pltpu.VMEM((count, *shape), jnp.bfloat16),
            pltpu.SemaphoreType.DMA((2 * -(-rows // ROW_BLOCK) + 2 + count,)),
        ],
        compiler_params=pltpu.CompilerParams(vmem_limit_bytes=ALL_VMEM_BYTES),
        cost_estimate=pl.CostEstimate(flops=SMALL_COST, bytes_accessed=SMALL_COST, transcendentals=0),
        name=f"spectra_{first}",
    )(me, *operands)


def channel_power(spectra, mixers_ref, high, low):
    frames, _, _, _, channels = spectra[0].shape
    beams = mixers_ref.shape[1] // 2
    step = min(frames, max(1, WIDE // channels))

    def group(first, count, over_frames):
        power = None
        for p in range(2):
            sides = []
            for side in range(count):
                parts = []
                for piece in spectra:
                    for r in range(2):
                        parts.append(piece[first + side, p, r])
                sides.append(jnp.concatenate(parts, axis=0))
            stacked = jnp.concatenate(sides, axis=1)
            voltage = jnp.dot(mixers_ref[p], stacked, preferred_element_type=jnp.float32)
            real_part, imag_part = voltage[:beams], voltage[beams:]
            term = real_part * real_part + imag_part * imag_part
            power = term if power is None else power + term
        upper = power.astype(jnp.bfloat16)
        at = first * channels if isinstance(first, int) else pl.multiple_of(first * channels, step * channels)
        high[:, pl.ds(at, count * channels)] = upper
        low[:, pl.ds(at, count * channels)] = (power - upper.astype(jnp.float32)).astype(jnp.bfloat16)
        for side in range(count):
            over_frames = over_frames + power[:, side * channels : (side + 1) * channels]
        return over_frames

    whole = frames // step
    over_frames = jnp.zeros((beams, channels), jnp.float32)
    for i in range(whole):
        over_frames = group(i * step, step, over_frames)
    if frames > whole * step:
        over_frames = group(whole * step, frames - whole * step, over_frames)
    return over_frames


def placed(high, low, place_ref):
    total = jnp.dot(high[...], place_ref[...], preferred_element_type=jnp.float32)
    return total + jnp.dot(low[...], place_ref[...], preferred_element_type=jnp.float32)


def first_kernel(pieces, *refs):
    spectra, (mixers_ref, place_ref, sums_ref, level_ref, high, low) = refs[:pieces], refs[pieces:]
    level_ref[...] = channel_power(spectra, mixers_ref, high, low).astype(jnp.bfloat16)
    sums_ref[...] = placed(high, low, place_ref)


def last_kernel(pieces, levels, level_scale, *refs):
    spectra, refs = refs[:pieces], refs[pieces:]
    level_refs, refs = refs[:levels], refs[levels:]
    mixers_ref, place_ref, centre_ref, earlier_ref, out, high, low = refs
    channel_power(spectra, mixers_ref, high, low)
    level = level_refs[0][...].astype(jnp.float32)
    for ref in level_refs[1:]:
        level = level + ref[...].astype(jnp.float32)
    level = (level * level_scale).astype(jnp.bfloat16)
    total = earlier_ref[...] - jnp.dot(level, centre_ref[...], preferred_element_type=jnp.float32)
    total = total + placed(high, low, place_ref)
    blocks, width, share = out.shape
    groups = total.shape[1] // width
    for block in range(blocks):
        row, column = block // groups * share, block % groups * width
        out[block] = total[row : row + share, column : column + width].T.astype(jnp.bfloat16)


def beam_call(kernel, name, out_shape, spectra, mixers, *rest):
    frames, _, _, _, channels = spectra[0].shape
    beams = mixers.shape[1] // 2
    operands = [*spectra, *rest]
    return pl.pallas_call(
        kernel,
        out_shape=out_shape,
        in_specs=[vmem_spec()] * len(operands),
        out_specs=jax.tree.map(lambda _: vmem_spec(), out_shape),
        scratch_shapes=[pltpu.VMEM((beams, frames * channels), jnp.bfloat16)] * 2,
        compiler_params=pltpu.CompilerParams(vmem_limit_bytes=VMEM_BYTES),
        cost_estimate=pl.CostEstimate(flops=SMALL_COST, bytes_accessed=SMALL_COST, transcendentals=0),
        name=name,
    )(*operands)


def tables_kernel(total, *refs):
    where_ref, order_ref, weights_ref, delay_ref, mixers_ref, place_ref, centre_ref = refs
    time = where_ref[0]
    stations = weights_ref.shape[1]
    beams = mixers_ref.shape[1] // 2
    inputs = mixers_ref.shape[2]
    station = lax.broadcasted_iota(jnp.int32, (stations, inputs), 0)
    imag_column = order_ref[2:3, :] == 1
    for p in range(2):
        select = (station == order_ref[p : p + 1, :]).astype(jnp.bfloat16)
        picked = []
        for r in range(2):
            picked.append(
                lax.dot_general(
                    weights_ref[r], select, (((0,), (0,)), ((), ())), preferred_element_type=jnp.float32
                )
            )
        real_part, imag_part = picked
        mixers_ref[p, :beams, :] = jnp.where(imag_column, -imag_part, real_part).astype(jnp.bfloat16)
        mixers_ref[p, beams:, :] = jnp.where(imag_column, real_part, imag_part).astype(jnp.bfloat16)
    channels, curves = delay_ref.shape
    frames, _, width = place_ref.shape
    lane = lax.broadcasted_iota(jnp.int32, (1, width), 1)
    curve = lane // frames % curves
    wanted = lane // (frames * curves) * frames + lane % frames
    source = jnp.broadcast_to(wanted, (channels, width))
    for d in range(curves):
        source = source + jnp.where(curve == d, delay_ref[:, d : d + 1], 0)
    base = jnp.where(source < total, 1.0 / total, 0.0)
    for f in range(frames):
        hit = jnp.where(source == time * frames + f, 1.0, 0.0)
        place_ref[f] = (hit - base).astype(jnp.bfloat16)
    held = jnp.where((source >= time * frames) & (source < (time + 1) * frames), 1.0, 0.0)
    centre_ref[...] = (held - base * frames).astype(jnp.bfloat16)


def make_tables(beam_weights, station_index, delay_table, in_dev, frames_dev):
    chan_devices = lax.axis_size("chan")
    beam_devices = lax.axis_size("beam")
    time_devices = lax.axis_size("tm")
    here, core = lax.axis_index("chan"), lax.axis_index("beam")
    stations = beam_weights.shape[0]
    arranged = jnp.transpose(beam_weights, (1, 0, 2)).reshape(2, stations, chan_devices, beam_devices, -1)
    chosen = lax.dynamic_index_in_dim(arranged, core, 3, keepdims=False)
    chosen = chosen.reshape(2, stations, -1)
    order = station_index.reshape(chan_devices, beam_devices, in_dev // 2, 2)
    order = picked_blocks(order, 0, [source_of(here, d, chan_devices) for d in range(chan_devices)])
    order = picked_blocks(order, 1, [source_of(core, e, beam_devices) for e in range(beam_devices)])
    order = jnp.transpose(order, (3, 0, 1, 2))
    order = jnp.broadcast_to(order[:, :, :, None, :], (*order.shape[:3], 2, in_dev // 2)).reshape(2, -1)
    imag_column = jnp.arange(order.shape[1], dtype=jnp.int32) // (in_dev // 2) % 2
    order = jnp.concatenate([order, imag_column[None]], axis=0)
    where = lax.axis_index("tm").astype(jnp.int32).reshape(1)
    channels, curves = delay_table.shape
    beams = chosen.shape[2]
    inputs = order.shape[1]
    width = time_devices * curves * frames_dev
    return pl.pallas_call(
        functools.partial(tables_kernel, time_devices * frames_dev),
        out_shape=[
            jax.ShapeDtypeStruct((2, 2 * beams, inputs), jnp.bfloat16),
            jax.ShapeDtypeStruct((frames_dev, channels, width), jnp.bfloat16),
            jax.ShapeDtypeStruct((channels, width), jnp.bfloat16),
        ],
        in_specs=[pl.BlockSpec(memory_space=pltpu.SMEM)] + [vmem_spec()] * 3,
        out_specs=[vmem_spec()] * 3,
        compiler_params=pltpu.CompilerParams(vmem_limit_bytes=VMEM_BYTES),
        cost_estimate=pl.CostEstimate(flops=SMALL_COST, bytes_accessed=SMALL_COST, transcendentals=0),
        name="tables",
    )(where, order, chosen, delay_table)


def shards(voltages, filter_taps, beam_weights, station_index, delay_table):
    taps, length = filter_taps.shape
    in_dev = voltages.shape[0]
    frames_dev = voltages.shape[1] // length
    chan_devices = lax.axis_size("chan")
    beam_devices = lax.axis_size("beam")
    time_devices = lax.axis_size("tm")
    channels = delay_table.shape[0]
    curves = delay_table.shape[1]
    me = lax.axis_index("chan").astype(jnp.int32).reshape(1)
    dft = dft_blocks(length, chan_devices)
    history = taps - 1
    half = min(taps - 1, frames_dev // 2)
    rim = None
    ready = []
    for first, frames in ((half, frames_dev - half), (0, half)):
        emit = rim is None
        if not emit:
            rim, mixers, place, centre = lax.optimization_barrier((rim, mixers, place, centre))
        own = make_spectra(me, rim, voltages, filter_taps, dft, first, frames, emit)
        if emit:
            *own, rim = own
            rim = from_previous(rim, "tm")
            late, own[0] = lax.optimization_barrier(((beam_weights, station_index, delay_table), own[0]))
            mixers, place, centre = make_tables(*late, in_dev, frames_dev)
            place = place.reshape(frames_dev * channels, -1)
        ready.append([own[0]] + [exchanged(own[d], "chan", d) for d in range(1, chan_devices)])
    ready[0], ready[1][0] = lax.optimization_barrier((ready[0], ready[1][0]))

    def with_hops(arrived):
        pieces = []
        for here in arrived:
            pieces += [here] + [exchanged(here, "beam", e) for e in range(1, beam_devices)]
        return pieces

    beams = mixers.shape[1] // 2
    spectra = with_hops(ready[0])
    shapes = [
        jax.ShapeDtypeStruct((beams, place.shape[1]), jnp.float32),
        jax.ShapeDtypeStruct((beams, channels), jnp.bfloat16),
    ]
    sums, level = beam_call(
        functools.partial(first_kernel, len(spectra)),
        "beam_first",
        shapes,
        spectra,
        mixers,
        mixers,
        place[half * channels :],
    )
    levels = [level] + [exchanged(level, "tm", e) for e in range(1, time_devices)]
    ready[1], sums, levels = lax.optimization_barrier((ready[1], sums, levels))
    spectra = with_hops(ready[1])
    level_scale = 1.0 / (time_devices * (frames_dev - half))
    share = beams // chan_devices
    blocks = beam_call(
        functools.partial(last_kernel, len(spectra), len(levels), level_scale),
        "beam_last",
        jax.ShapeDtypeStruct((chan_devices * time_devices, curves * frames_dev, share), jnp.bfloat16),
        spectra,
        mixers,
        *levels,
        mixers,
        place[: half * channels],
        centre,
        sums,
    )
    blocks = lax.all_to_all(blocks, ("chan", "tm"), split_axis=0, concat_axis=0, tiled=True)
    final = jnp.sum(blocks.astype(jnp.float32), axis=0)
    final = final * (1.0 / math.sqrt(length // 2))
    return jnp.transpose(final.reshape(curves, frames_dev, share), (2, 0, 1))


def solution(mesh):
    in_specs = (P(("groups", "chan", "beam"), "tm"), P(), P(), P(), P("chan", None))
    out_specs = P(("groups", "chan", "beam"), None, "tm")
    return jax.shard_map(shards, mesh=mesh, in_specs=in_specs, out_specs=out_specs, check_vma=False)
```

```python
import functools
import math

import jax
import jax.numpy as jnp
import numpy as np
from jax import lax
from jax.experimental import pallas as pl
from jax.experimental.pallas import tpu as pltpu
from jax.sharding import PartitionSpec as P

VMEM_BYTES = 24 << 20
ALL_VMEM_BYTES = 60 << 20
LANES = 128
SMALL_COST = 1024
WIDE = 256
ROW_BLOCK = 32


def partner(index, step, count):
    return index ^ (-step % count) if count & (count - 1) == 0 else (index + step) % count


def source_of(index, step, count):
    return index ^ (-step % count) if count & (count - 1) == 0 else (index - step) % count


def exchanged(value, axis, step):
    count = lax.axis_size(axis)
    return lax.ppermute(value, axis, [(source, partner(source, step, count)) for source in range(count)])


def picked_blocks(value, axis, indices):
    return jnp.concatenate([lax.dynamic_slice_in_dim(value, i, 1, axis) for i in indices], axis=axis)


def from_previous(value, axis):
    count = lax.axis_size(axis)
    return lax.ppermute(value, axis, [(source, source + 1) for source in range(count - 1)])


def dft_blocks(length, blocks):
    channels = length // 2
    phase = (np.arange(length)[:, None] * np.arange(channels)[None, :] % length) * (2.0 * math.pi / length)
    table = np.stack([np.cos(phase), -np.sin(phase)], axis=1).reshape(length, 2, blocks, channels // blocks)
    return jnp.asarray(np.transpose(table, (2, 0, 1, 3)).reshape(blocks, length, -1), jnp.bfloat16)


def vmem_spec():
    return pl.BlockSpec(memory_space=pltpu.VMEM)


def spectra_kernel(first, frames, length, has_rim, emit, *refs):
    me_ref, refs = refs[0], refs[1:]
    rim_hbm, refs = (refs[0], refs[1:]) if has_rim else (None, refs)
    volt_hbm, taps_hbm, dft_hbm = refs[:3]
    outs, (volt, taps_ref, dft_ref, filt, spread, made, sems) = refs[3:-7], refs[-7:]
    taps = taps_ref.shape[0]
    rows = volt.shape[0]
    row_block = spread.shape[1]
    half = row_block // 2
    history = taps - 1

    taps_copy = pltpu.make_async_copy(taps_hbm, taps_ref, sems.at[0])
    taps_copy.start()
    early = max(0, history - first)
    sources = [(volt_hbm, max(0, first - history) * length, early * length, (history + frames - early) * length)]
    if has_rim:
        sources.append((rim_hbm, (history - early) * length, 0, early * length))
    copies = []
    for block in range(rows // row_block):
        span = pl.ds(block * row_block, row_block)
        for n, (source, start, at, size) in enumerate(sources):
            copies.append(
                pltpu.make_async_copy(
                    source.at[span, pl.ds(start, size)],
                    volt.at[span, pl.ds(at, size)],
                    sems.at[2 + block * len(sources) + n],
                )
            )
            copies[-1].start()
    table_copy = pltpu.make_async_copy(dft_hbm, dft_ref, sems.at[1])
    writes = []
    if emit:
        *outs, rim_out = outs

    def filtered_block(block):
        row = block * row_block

        def columns(n, _):
            lane = pl.multiple_of(n * LANES, LANES)
            weights = [taps_ref[t : t + 1, pl.ds(lane, LANES)] for t in range(taps)]

            def load(slot):
                at = pl.multiple_of(slot * length + lane, LANES)
                return volt[row : row + row_block, pl.ds(at, LANES)].astype(jnp.float32)

            window = [load(t) for t in range(history)]
            for f in range(frames):
                window.append(load(f + history))
                total = weights[0] * window[0]
                for t in range(1, taps):
                    total = total + weights[t] * window[t]
                window.pop(0)
                slot = f % spread.shape[0]
                spread[slot] = total
                for p in range(2):
                    picked = spread[slot, pl.ds(p, half, stride=2), :]
                    filt[pl.ds((f * 2 + p) * (rows // 2) + row // 2, half), pl.ds(lane, LANES)] = picked.astype(
                        jnp.bfloat16
                    )
            return 0

        lax.fori_loop(0, length // LANES, columns, 0)

    for block in range(rows // row_block):
        for copy in copies[block * len(sources) : (block + 1) * len(sources)]:
            copy.wait()
        if block == 0:
            taps_copy.wait()
            table_copy.start()
        filtered_block(block)
    if emit:
        writes.append(
            pltpu.make_async_copy(volt.at[:, pl.ds(frames * length, history * length)], rim_out, sems.at[2])
        )
        writes[-1].start()
    table_copy.wait()
    count = dft_ref.shape[0]
    stations = rows // 2
    channels = outs[0].shape[-1]
    for d in (*range(1, count), 0):
        block = partner(me_ref[0], d, count)
        result = jnp.dot(filt[...], dft_ref[block], preferred_element_type=jnp.float32).astype(jnp.bfloat16)
        for f in range(frames):
            for p in range(2):
                at = (f * 2 + p) * stations
                for r in range(2):
                    made[d, f, p, r] = result[at : at + stations, r * channels : (r + 1) * channels]
        writes.append(pltpu.make_async_copy(made.at[d], outs[d], sems.at[sems.shape[0] - 1 - d]))
        writes[-1].start()
    for write in writes:
        write.wait()


def make_spectra(me, rim, voltages, filter_taps, dft, first, frames, emit):
    rows = voltages.shape[0]
    taps, length = filter_taps.shape
    count = dft.shape[0]
    channels = dft.shape[2] // 2
    has_rim = rim is not None
    operands = ([rim] if has_rim else []) + [voltages, filter_taps, dft]
    shape = (frames, 2, 2, rows // 2, channels)
    slots = frames + taps - 1
    return pl.pallas_call(
        functools.partial(spectra_kernel, first, frames, length, has_rim, emit),
        out_shape=[jax.ShapeDtypeStruct(shape, jnp.bfloat16)] * count
        + [jax.ShapeDtypeStruct((rows, (taps - 1) * length), jnp.bfloat16)] * emit,
        in_specs=[pl.BlockSpec(memory_space=pltpu.SMEM)] + [pl.BlockSpec(memory_space=pl.ANY)] * len(operands),
        out_specs=[pl.BlockSpec(memory_space=pl.ANY)] * (count + emit),
        scratch_shapes=[
            pltpu.VMEM((rows, slots * length), jnp.bfloat16),
            pltpu.VMEM((taps, length), jnp.float32),
            pltpu.VMEM(dft.shape, jnp.bfloat16),
            pltpu.VMEM((frames * rows, length), jnp.bfloat16),
            pltpu.VMEM((8, min(rows, ROW_BLOCK), LANES), jnp.float32),
            pltpu.VMEM((count, *shape), jnp.bfloat16),
            pltpu.SemaphoreType.DMA((2 * -(-rows // ROW_BLOCK) + 2 + count,)),
        ],
        compiler_params=pltpu.CompilerParams(vmem_limit_bytes=ALL_VMEM_BYTES),
        cost_estimate=pl.CostEstimate(flops=SMALL_COST, bytes_accessed=SMALL_COST, transcendentals=0),
        name=f"spectra_{first}",
    )(me, *operands)


def channel_power(spectra, mixers_ref, high, low):
    frames, _, _, _, channels = spectra[0].shape
    beams = mixers_ref.shape[1] // 2
    step = min(frames, max(1, WIDE // channels))

    def group(first, count, over_frames):
        power = None
        for p in range(2):
            sides = []
            for side in range(count):
                parts = []
                for piece in spectra:
                    for r in range(2):
                        parts.append(piece[first + side, p, r])
                sides.append(jnp.concatenate(parts, axis=0))
            stacked = jnp.concatenate(sides, axis=1)
            voltage = jnp.dot(mixers_ref[p], stacked, preferred_element_type=jnp.float32)
            real_part, imag_part = voltage[:beams], voltage[beams:]
            term = real_part * real_part + imag_part * imag_part
            power = term if power is None else power + term
        upper = power.astype(jnp.bfloat16)
        at = first * channels if isinstance(first, int) else pl.multiple_of(first * channels, step * channels)
        high[:, pl.ds(at, count * channels)] = upper
        low[:, pl.ds(at, count * channels)] = (power - upper.astype(jnp.float32)).astype(jnp.bfloat16)
        for side in range(count):
            over_frames = over_frames + power[:, side * channels : (side + 1) * channels]
        return over_frames

    whole = frames // step
    over_frames = jnp.zeros((beams, channels), jnp.float32)
    for i in range(whole):
        over_frames = group(i * step, step, over_frames)
    if frames > whole * step:
        over_frames = group(whole * step, frames - whole * step, over_frames)
    return over_frames


def placed(high, low, place_ref):
    total = jnp.dot(high[...], place_ref[...], preferred_element_type=jnp.float32)
    return total + jnp.dot(low[...], place_ref[...], preferred_element_type=jnp.float32)


def first_kernel(pieces, *refs):
    spectra, (mixers_ref, place_ref, sums_ref, level_ref, high, low) = refs[:pieces], refs[pieces:]
    level_ref[...] = channel_power(spectra, mixers_ref, high, low).astype(jnp.bfloat16)
    sums_ref[...] = placed(high, low, place_ref)


def last_kernel(pieces, levels, level_scale, *refs):
    spectra, refs = refs[:pieces], refs[pieces:]
    level_refs, refs = refs[:levels], refs[levels:]
    mixers_ref, place_ref, centre_ref, earlier_ref, out, high, low = refs
    channel_power(spectra, mixers_ref, high, low)
    level = level_refs[0][...].astype(jnp.float32)
    for ref in level_refs[1:]:
        level = level + ref[...].astype(jnp.float32)
    level = (level * level_scale).astype(jnp.bfloat16)
    total = earlier_ref[...] - jnp.dot(level, centre_ref[...], preferred_element_type=jnp.float32)
    total = total + placed(high, low, place_ref)
    blocks, width, share = out.shape
    groups = total.shape[1] // width
    for block in range(blocks):
        row, column = block // groups * share, block % groups * width
        out[block] = total[row : row + share, column : column + width].T.astype(jnp.bfloat16)


def beam_call(kernel, name, out_shape, spectra, mixers, *rest):
    frames, _, _, _, channels = spectra[0].shape
    beams = mixers.shape[1] // 2
    operands = [*spectra, *rest]
    return pl.pallas_call(
        kernel,
        out_shape=out_shape,
        in_specs=[vmem_spec()] * len(operands),
        out_specs=jax.tree.map(lambda _: vmem_spec(), out_shape),
        scratch_shapes=[pltpu.VMEM((beams, frames * channels), jnp.bfloat16)] * 2,
        compiler_params=pltpu.CompilerParams(vmem_limit_bytes=VMEM_BYTES),
        cost_estimate=pl.CostEstimate(flops=SMALL_COST, bytes_accessed=SMALL_COST, transcendentals=0),
        name=name,
    )(*operands)


def tables_kernel(total, *refs):
    where_ref, order_ref, weights_ref, delay_ref, mixers_ref, place_ref, centre_ref = refs
    time = where_ref[0]
    stations = weights_ref.shape[1]
    beams = mixers_ref.shape[1] // 2
    inputs = mixers_ref.shape[2]
    station = lax.broadcasted_iota(jnp.int32, (stations, inputs), 0)
    imag_column = order_ref[2:3, :] == 1
    for p in range(2):
        select = (station == order_ref[p : p + 1, :]).astype(jnp.bfloat16)
        picked = []
        for r in range(2):
            picked.append(
                lax.dot_general(
                    weights_ref[r], select, (((0,), (0,)), ((), ())), preferred_element_type=jnp.float32
                )
            )
        real_part, imag_part = picked
        mixers_ref[p, :beams, :] = jnp.where(imag_column, -imag_part, real_part).astype(jnp.bfloat16)
        mixers_ref[p, beams:, :] = jnp.where(imag_column, real_part, imag_part).astype(jnp.bfloat16)
    channels, curves = delay_ref.shape
    frames, _, width = place_ref.shape
    lane = lax.broadcasted_iota(jnp.int32, (1, width), 1)
    curve = lane // frames % curves
    wanted = lane // (frames * curves) * frames + lane % frames
    source = jnp.broadcast_to(wanted, (channels, width))
    for d in range(curves):
        source = source + jnp.where(curve == d, delay_ref[:, d : d + 1], 0)
    base = jnp.where(source < total, 1.0 / total, 0.0)
    for f in range(frames):
        hit = jnp.where(source == time * frames + f, 1.0, 0.0)
        place_ref[f] = (hit - base).astype(jnp.bfloat16)
    held = jnp.where((source >= time * frames) & (source < (time + 1) * frames), 1.0, 0.0)
    centre_ref[...] = (held - base * frames).astype(jnp.bfloat16)


def make_tables(beam_weights, station_index, delay_table, in_dev, frames_dev):
    chan_devices = lax.axis_size("chan")
    beam_devices = lax.axis_size("beam")
    time_devices = lax.axis_size("tm")
    here, core = lax.axis_index("chan"), lax.axis_index("beam")
    stations = beam_weights.shape[0]
    arranged = jnp.transpose(beam_weights, (1, 0, 2)).reshape(2, stations, chan_devices, beam_devices, -1)
    chosen = lax.dynamic_index_in_dim(arranged, core, 3, keepdims=False)
    chosen = chosen.reshape(2, stations, -1)
    order = station_index.reshape(chan_devices, beam_devices, in_dev // 2, 2)
    order = picked_blocks(order, 0, [source_of(here, d, chan_devices) for d in range(chan_devices)])
    order = picked_blocks(order, 1, [source_of(core, e, beam_devices) for e in range(beam_devices)])
    order = jnp.transpose(order, (3, 0, 1, 2))
    order = jnp.broadcast_to(order[:, :, :, None, :], (*order.shape[:3], 2, in_dev // 2)).reshape(2, -1)
    imag_column = jnp.arange(order.shape[1], dtype=jnp.int32) // (in_dev // 2) % 2
    order = jnp.concatenate([order, imag_column[None]], axis=0)
    where = lax.axis_index("tm").astype(jnp.int32).reshape(1)
    channels, curves = delay_table.shape
    beams = chosen.shape[2]
    inputs = order.shape[1]
    width = time_devices * curves * frames_dev
    return pl.pallas_call(
        functools.partial(tables_kernel, time_devices * frames_dev),
        out_shape=[
            jax.ShapeDtypeStruct((2, 2 * beams, inputs), jnp.bfloat16),
            jax.ShapeDtypeStruct((frames_dev, channels, width), jnp.bfloat16),
            jax.ShapeDtypeStruct((channels, width), jnp.bfloat16),
        ],
        in_specs=[pl.BlockSpec(memory_space=pltpu.SMEM)] + [vmem_spec()] * 3,
        out_specs=[vmem_spec()] * 3,
        compiler_params=pltpu.CompilerParams(vmem_limit_bytes=VMEM_BYTES),
        cost_estimate=pl.CostEstimate(flops=SMALL_COST, bytes_accessed=SMALL_COST, transcendentals=0),
        name="tables",
    )(where, order, chosen, delay_table)


def shards(voltages, filter_taps, beam_weights, station_index, delay_table):
    taps, length = filter_taps.shape
    in_dev = voltages.shape[0]
    frames_dev = voltages.shape[1] // length
    chan_devices = lax.axis_size("chan")
    beam_devices = lax.axis_size("beam")
    time_devices = lax.axis_size("tm")
    channels = delay_table.shape[0]
    curves = delay_table.shape[1]
    me = lax.axis_index("chan").astype(jnp.int32).reshape(1)
    dft = dft_blocks(length, chan_devices)
    history = taps - 1
    half = min(taps - 1, frames_dev // 2)
    rim = None
    ready = []
    for first, frames in ((half, frames_dev - half), (0, half)):
        emit = rim is None
        if not emit:
            rim, mixers, place, centre = lax.optimization_barrier((rim, mixers, place, centre))
        own = make_spectra(me, rim, voltages, filter_taps, dft, first, frames, emit)
        if emit:
            *own, rim = own
            rim = from_previous(rim, "tm")
            late, own[0] = lax.optimization_barrier(((beam_weights, station_index, delay_table), own[0]))
            mixers, place, centre = make_tables(*late, in_dev, frames_dev)
            place = place.reshape(frames_dev * channels, -1)
        ready.append([own[0]] + [exchanged(own[d], "chan", d) for d in range(1, chan_devices)])
    ready[0][1:], ready[1][0] = lax.optimization_barrier((ready[0][1:], ready[1][0]))

    def with_hops(arrived):
        pieces = []
        for here in arrived:
            pieces += [here] + [exchanged(here, "beam", e) for e in range(1, beam_devices)]
        return pieces

    beams = mixers.shape[1] // 2
    spectra = with_hops(ready[0])
    shapes = [
        jax.ShapeDtypeStruct((beams, place.shape[1]), jnp.float32),
        jax.ShapeDtypeStruct((beams, channels), jnp.bfloat16),
    ]
    sums, level = beam_call(
        functools.partial(first_kernel, len(spectra)),
        "beam_first",
        shapes,
        spectra,
        mixers,
        mixers,
        place[half * channels :],
    )
    levels = [level] + [exchanged(level, "tm", e) for e in range(1, time_devices)]
    ready[1][1:], sums, levels = lax.optimization_barrier((ready[1][1:], sums, levels))
    spectra = with_hops(ready[1])
    level_scale = 1.0 / (time_devices * (frames_dev - half))
    share = beams // chan_devices
    blocks = beam_call(
        functools.partial(last_kernel, len(spectra), len(levels), level_scale),
        "beam_last",
        jax.ShapeDtypeStruct((chan_devices * time_devices, curves * frames_dev, share), jnp.bfloat16),
        spectra,
        mixers,
        *levels,
        mixers,
        place[: half * channels],
        centre,
        sums,
    )
    blocks = lax.all_to_all(blocks, ("chan", "tm"), split_axis=0, concat_axis=0, tiled=True)
    final = jnp.sum(blocks.astype(jnp.float32), axis=0)
    final = final * (1.0 / math.sqrt(length // 2))
    return jnp.transpose(final.reshape(curves, frames_dev, share), (2, 0, 1))


def solution(mesh):
    in_specs = (P(("groups", "chan", "beam"), "tm"), P(), P(), P(), P("chan", None))
    out_specs = P(("groups", "chan", "beam"), None, "tm")
    return jax.shard_map(shards, mesh=mesh, in_specs=in_specs, out_specs=out_specs, check_vma=False)
```

```python
import functools
import math

import jax
import jax.numpy as jnp
import numpy as np
from jax import lax
from jax.experimental import pallas as pl
from jax.experimental.pallas import tpu as pltpu
from jax.sharding import PartitionSpec as P

VMEM_BYTES = 24 << 20
ALL_VMEM_BYTES = 60 << 20
LANES = 128
SMALL_COST = 1024
WIDE = 256
ROW_BLOCK = 32


def partner(index, step, count):
    return index ^ (-step % count) if count & (count - 1) == 0 else (index + step) % count


def source_of(index, step, count):
    return index ^ (-step % count) if count & (count - 1) == 0 else (index - step) % count


def exchanged(value, axis, step):
    count = lax.axis_size(axis)
    return lax.ppermute(value, axis, [(source, partner(source, step, count)) for source in range(count)])


def picked_blocks(value, axis, indices):
    return jnp.concatenate([lax.dynamic_slice_in_dim(value, i, 1, axis) for i in indices], axis=axis)


def from_previous(value, axis):
    count = lax.axis_size(axis)
    return lax.ppermute(value, axis, [(source, source + 1) for source in range(count - 1)])


def dft_blocks(length, blocks):
    channels = length // 2
    phase = (np.arange(length)[:, None] * np.arange(channels)[None, :] % length) * (2.0 * math.pi / length)
    table = np.stack([np.cos(phase), -np.sin(phase)], axis=1).reshape(length, 2, blocks, channels // blocks)
    return jnp.asarray(np.transpose(table, (2, 0, 1, 3)).reshape(blocks, length, -1), jnp.bfloat16)


def vmem_spec():
    return pl.BlockSpec(memory_space=pltpu.VMEM)


def spectra_kernel(first, frames, length, has_rim, emit, *refs):
    me_ref, refs = refs[0], refs[1:]
    rim_hbm, refs = (refs[0], refs[1:]) if has_rim else (None, refs)
    volt_hbm, taps_hbm, dft_hbm = refs[:3]
    outs, (volt, taps_ref, dft_ref, filt, spread, made, sems) = refs[3:-7], refs[-7:]
    taps = taps_ref.shape[0]
    rows = volt.shape[0]
    row_block = spread.shape[1]
    half = row_block // 2
    history = taps - 1

    taps_copy = pltpu.make_async_copy(taps_hbm, taps_ref, sems.at[0])
    taps_copy.start()
    early = max(0, history - first)
    sources = [(volt_hbm, max(0, first - history) * length, early * length, (history + frames - early) * length)]
    if has_rim:
        sources.append((rim_hbm, (history - early) * length, 0, early * length))
    copies = []
    for block in range(rows // row_block):
        span = pl.ds(block * row_block, row_block)
        for n, (source, start, at, size) in enumerate(sources):
            copies.append(
                pltpu.make_async_copy(
                    source.at[span, pl.ds(start, size)],
                    volt.at[span, pl.ds(at, size)],
                    sems.at[2 + block * len(sources) + n],
                )
            )
            copies[-1].start()
    count = dft_ref.shape[0]
    steps = (*range(1, count), 0)
    table_copies = []
    for d in steps:
        block = partner(me_ref[0], d, count)
        table_copies.append(
            pltpu.make_async_copy(dft_hbm.at[block], dft_ref.at[block], sems.at[sems.shape[0] - 1 - d])
        )
    writes = []
    if emit:
        *outs, rim_out = outs

    def filtered_block(block):
        row = block * row_block

        def columns(n, _):
            lane = pl.multiple_of(n * LANES, LANES)
            weights = [taps_ref[t : t + 1, pl.ds(lane, LANES)] for t in range(taps)]

            def load(slot):
                at = pl.multiple_of(slot * length + lane, LANES)
                return volt[row : row + row_block, pl.ds(at, LANES)].astype(jnp.float32)

            window = [load(t) for t in range(history)]
            for f in range(frames):
                window.append(load(f + history))
                total = weights[0] * window[0]
                for t in range(1, taps):
                    total = total + weights[t] * window[t]
                window.pop(0)
                slot = f % spread.shape[0]
                spread[slot] = total
                for p in range(2):
                    picked = spread[slot, pl.ds(p, half, stride=2), :]
                    filt[pl.ds((f * 2 + p) * (rows // 2) + row // 2, half), pl.ds(lane, LANES)] = picked.astype(
                        jnp.bfloat16
                    )
            return 0

        lax.fori_loop(0, length // LANES, columns, 0)

    for block in range(rows // row_block):
        for copy in copies[block * len(sources) : (block + 1) * len(sources)]:
            copy.wait()
        if block == 0:
            taps_copy.wait()
            for table_copy in table_copies:
                table_copy.start()
        filtered_block(block)
    if emit:
        writes.append(
            pltpu.make_async_copy(volt.at[:, pl.ds(frames * length, history * length)], rim_out, sems.at[2])
        )
        writes[-1].start()
    for table_copy in table_copies:
        table_copy.wait()
    stations = rows // 2
    channels = outs[0].shape[-1]
    for d in steps:
        block = partner(me_ref[0], d, count)
        result = jnp.dot(filt[...], dft_ref[block], preferred_element_type=jnp.float32).astype(jnp.bfloat16)
        for f in range(frames):
            for p in range(2):
                at = (f * 2 + p) * stations
                for r in range(2):
                    made[d, f, p, r] = result[at : at + stations, r * channels : (r + 1) * channels]
        writes.append(pltpu.make_async_copy(made.at[d], outs[d], sems.at[sems.shape[0] - 1 - d]))
        writes[-1].start()
    for write in writes:
        write.wait()


def make_spectra(me, rim, voltages, filter_taps, dft, first, frames, emit):
    rows = voltages.shape[0]
    taps, length = filter_taps.shape
    count = dft.shape[0]
    channels = dft.shape[2] // 2
    has_rim = rim is not None
    operands = ([rim] if has_rim else []) + [voltages, filter_taps, dft]
    shape = (frames, 2, 2, rows // 2, channels)
    slots = frames + taps - 1
    return pl.pallas_call(
        functools.partial(spectra_kernel, first, frames, length, has_rim, emit),
        out_shape=[jax.ShapeDtypeStruct(shape, jnp.bfloat16)] * count
        + [jax.ShapeDtypeStruct((rows, (taps - 1) * length), jnp.bfloat16)] * emit,
        in_specs=[pl.BlockSpec(memory_space=pltpu.SMEM)] + [pl.BlockSpec(memory_space=pl.ANY)] * len(operands),
        out_specs=[pl.BlockSpec(memory_space=pl.ANY)] * (count + emit),
        scratch_shapes=[
            pltpu.VMEM((rows, slots * length), jnp.bfloat16),
            pltpu.VMEM((taps, length), jnp.float32),
            pltpu.VMEM(dft.shape, jnp.bfloat16),
            pltpu.VMEM((frames * rows, length), jnp.bfloat16),
            pltpu.VMEM((8, min(rows, ROW_BLOCK), LANES), jnp.float32),
            pltpu.VMEM((count, *shape), jnp.bfloat16),
            pltpu.SemaphoreType.DMA((2 * -(-rows // ROW_BLOCK) + 2 + count,)),
        ],
        compiler_params=pltpu.CompilerParams(vmem_limit_bytes=ALL_VMEM_BYTES),
        cost_estimate=pl.CostEstimate(flops=SMALL_COST, bytes_accessed=SMALL_COST, transcendentals=0),
        name=f"spectra_{first}",
    )(me, *operands)


def channel_power(spectra, mixers_ref, high, low):
    frames, _, _, _, channels = spectra[0].shape
    beams = mixers_ref.shape[1] // 2
    step = min(frames, max(1, WIDE // channels))

    def group(first, count, over_frames):
        power = None
        for p in range(2):
            sides = []
            for side in range(count):
                parts = []
                for piece in spectra:
                    for r in range(2):
                        parts.append(piece[first + side, p, r])
                sides.append(jnp.concatenate(parts, axis=0))
            stacked = jnp.concatenate(sides, axis=1)
            voltage = jnp.dot(mixers_ref[p], stacked, preferred_element_type=jnp.float32)
            real_part, imag_part = voltage[:beams], voltage[beams:]
            term = real_part * real_part + imag_part * imag_part
            power = term if power is None else power + term
        upper = power.astype(jnp.bfloat16)
        at = first * channels if isinstance(first, int) else pl.multiple_of(first * channels, step * channels)
        high[:, pl.ds(at, count * channels)] = upper
        low[:, pl.ds(at, count * channels)] = (power - upper.astype(jnp.float32)).astype(jnp.bfloat16)
        for side in range(count):
            over_frames = over_frames + power[:, side * channels : (side + 1) * channels]
        return over_frames

    whole = frames // step
    over_frames = jnp.zeros((beams, channels), jnp.float32)
    for i in range(whole):
        over_frames = group(i * step, step, over_frames)
    if frames > whole * step:
        over_frames = group(whole * step, frames - whole * step, over_frames)
    return over_frames


def placed(high, low, place_ref):
    total = jnp.dot(high[...], place_ref[...], preferred_element_type=jnp.float32)
    return total + jnp.dot(low[...], place_ref[...], preferred_element_type=jnp.float32)


def first_kernel(pieces, *refs):
    spectra, (mixers_ref, place_ref, sums_ref, level_ref, high, low) = refs[:pieces], refs[pieces:]
    level_ref[...] = channel_power(spectra, mixers_ref, high, low).astype(jnp.bfloat16)
    sums_ref[...] = placed(high, low, place_ref)


def last_kernel(pieces, levels, level_scale, *refs):
    spectra, refs = refs[:pieces], refs[pieces:]
    level_refs, refs = refs[:levels], refs[levels:]
    mixers_ref, place_ref, centre_ref, earlier_ref, out, high, low = refs
    channel_power(spectra, mixers_ref, high, low)
    level = level_refs[0][...].astype(jnp.float32)
    for ref in level_refs[1:]:
        level = level + ref[...].astype(jnp.float32)
    level = (level * level_scale).astype(jnp.bfloat16)
    total = earlier_ref[...] - jnp.dot(level, centre_ref[...], preferred_element_type=jnp.float32)
    total = total + placed(high, low, place_ref)
    blocks, width, share = out.shape
    groups = total.shape[1] // width
    for block in range(blocks):
        row, column = block // groups * share, block % groups * width
        out[block] = total[row : row + share, column : column + width].T.astype(jnp.bfloat16)


def beam_call(kernel, name, out_shape, spectra, mixers, *rest):
    frames, _, _, _, channels = spectra[0].shape
    beams = mixers.shape[1] // 2
    operands = [*spectra, *rest]
    return pl.pallas_call(
        kernel,
        out_shape=out_shape,
        in_specs=[vmem_spec()] * len(operands),
        out_specs=jax.tree.map(lambda _: vmem_spec(), out_shape),
        scratch_shapes=[pltpu.VMEM((beams, frames * channels), jnp.bfloat16)] * 2,
        compiler_params=pltpu.CompilerParams(vmem_limit_bytes=VMEM_BYTES),
        cost_estimate=pl.CostEstimate(flops=SMALL_COST, bytes_accessed=SMALL_COST, transcendentals=0),
        name=name,
    )(*operands)


def tables_kernel(total, *refs):
    where_ref, order_ref, weights_ref, delay_ref, mixers_ref, place_ref, centre_ref = refs
    time = where_ref[0]
    stations = weights_ref.shape[1]
    beams = mixers_ref.shape[1] // 2
    inputs = mixers_ref.shape[2]
    station = lax.broadcasted_iota(jnp.int32, (stations, inputs), 0)
    imag_column = order_ref[2:3, :] == 1
    for p in range(2):
        select = (station == order_ref[p : p + 1, :]).astype(jnp.bfloat16)
        picked = []
        for r in range(2):
            picked.append(
                lax.dot_general(
                    weights_ref[r], select, (((0,), (0,)), ((), ())), preferred_element_type=jnp.float32
                )
            )
        real_part, imag_part = picked
        mixers_ref[p, :beams, :] = jnp.where(imag_column, -imag_part, real_part).astype(jnp.bfloat16)
        mixers_ref[p, beams:, :] = jnp.where(imag_column, real_part, imag_part).astype(jnp.bfloat16)
    channels, curves = delay_ref.shape
    frames, _, width = place_ref.shape
    lane = lax.broadcasted_iota(jnp.int32, (1, width), 1)
    curve = lane // frames % curves
    wanted = lane // (frames * curves) * frames + lane % frames
    source = jnp.broadcast_to(wanted, (channels, width))
    for d in range(curves):
        source = source + jnp.where(curve == d, delay_ref[:, d : d + 1], 0)
    base = jnp.where(source < total, 1.0 / total, 0.0)
    for f in range(frames):
        hit = jnp.where(source == time * frames + f, 1.0, 0.0)
        place_ref[f] = (hit - base).astype(jnp.bfloat16)
    held = jnp.where((source >= time * frames) & (source < (time + 1) * frames), 1.0, 0.0)
    centre_ref[...] = (held - base * frames).astype(jnp.bfloat16)


def make_tables(beam_weights, station_index, delay_table, in_dev, frames_dev):
    chan_devices = lax.axis_size("chan")
    beam_devices = lax.axis_size("beam")
    time_devices = lax.axis_size("tm")
    here, core = lax.axis_index("chan"), lax.axis_index("beam")
    stations = beam_weights.shape[0]
    arranged = jnp.transpose(beam_weights, (1, 0, 2)).reshape(2, stations, chan_devices, beam_devices, -1)
    chosen = lax.dynamic_index_in_dim(arranged, core, 3, keepdims=False)
    chosen = chosen.reshape(2, stations, -1)
    order = station_index.reshape(chan_devices, beam_devices, in_dev // 2, 2)
    order = picked_blocks(order, 0, [source_of(here, d, chan_devices) for d in range(chan_devices)])
    order = picked_blocks(order, 1, [source_of(core, e, beam_devices) for e in range(beam_devices)])
    order = jnp.transpose(order, (3, 0, 1, 2))
    order = jnp.broadcast_to(order[:, :, :, None, :], (*order.shape[:3], 2, in_dev // 2)).reshape(2, -1)
    imag_column = jnp.arange(order.shape[1], dtype=jnp.int32) // (in_dev // 2) % 2
    order = jnp.concatenate([order, imag_column[None]], axis=0)
    where = lax.axis_index("tm").astype(jnp.int32).reshape(1)
    channels, curves = delay_table.shape
    beams = chosen.shape[2]
    inputs = order.shape[1]
    width = time_devices * curves * frames_dev
    return pl.pallas_call(
        functools.partial(tables_kernel, time_devices * frames_dev),
        out_shape=[
            jax.ShapeDtypeStruct((2, 2 * beams, inputs), jnp.bfloat16),
            jax.ShapeDtypeStruct((frames_dev, channels, width), jnp.bfloat16),
            jax.ShapeDtypeStruct((channels, width), jnp.bfloat16),
        ],
        in_specs=[pl.BlockSpec(memory_space=pltpu.SMEM)] + [vmem_spec()] * 3,
        out_specs=[vmem_spec()] * 3,
        compiler_params=pltpu.CompilerParams(vmem_limit_bytes=VMEM_BYTES),
        cost_estimate=pl.CostEstimate(flops=SMALL_COST, bytes_accessed=SMALL_COST, transcendentals=0),
        name="tables",
    )(where, order, chosen, delay_table)


def shards(voltages, filter_taps, beam_weights, station_index, delay_table):
    taps, length = filter_taps.shape
    in_dev = voltages.shape[0]
    frames_dev = voltages.shape[1] // length
    chan_devices = lax.axis_size("chan")
    beam_devices = lax.axis_size("beam")
    time_devices = lax.axis_size("tm")
    channels = delay_table.shape[0]
    curves = delay_table.shape[1]
    me = lax.axis_index("chan").astype(jnp.int32).reshape(1)
    dft = dft_blocks(length, chan_devices)
    history = taps - 1
    half = min(taps - 1, frames_dev // 2)
    rim = None
    ready = []
    for first, frames in ((half, frames_dev - half), (0, half)):
        emit = rim is None
        if not emit:
            rim, mixers, place, centre = lax.optimization_barrier((rim, mixers, place, centre))
        own = make_spectra(me, rim, voltages, filter_taps, dft, first, frames, emit)
        if emit:
            *own, rim = own
            rim = from_previous(rim, "tm")
            late, own[0] = lax.optimization_barrier(((beam_weights, station_index, delay_table), own[0]))
            mixers, place, centre = make_tables(*late, in_dev, frames_dev)
            place = place.reshape(frames_dev * channels, -1)
        ready.append([own[0]] + [exchanged(own[d], "chan", d) for d in range(1, chan_devices)])
    ready[0][1:], ready[1][0] = lax.optimization_barrier((ready[0][1:], ready[1][0]))

    def with_hops(arrived):
        pieces = []
        for here in arrived:
            pieces += [here] + [exchanged(here, "beam", e) for e in range(1, beam_devices)]
        return pieces

    beams = mixers.shape[1] // 2
    spectra = with_hops(ready[0])
    shapes = [
        jax.ShapeDtypeStruct((beams, place.shape[1]), jnp.float32),
        jax.ShapeDtypeStruct((beams, channels), jnp.bfloat16),
    ]
    sums, level = beam_call(
        functools.partial(first_kernel, len(spectra)),
        "beam_first",
        shapes,
        spectra,
        mixers,
        mixers,
        place[half * channels :],
    )
    levels = [level] + [exchanged(level, "tm", e) for e in range(1, time_devices)]
    ready[1][1:], sums, levels = lax.optimization_barrier((ready[1][1:], sums, levels))
    spectra = with_hops(ready[1])
    level_scale = 1.0 / (time_devices * (frames_dev - half))
    share = beams // chan_devices
    blocks = beam_call(
        functools.partial(last_kernel, len(spectra), len(levels), level_scale),
        "beam_last",
        jax.ShapeDtypeStruct((chan_devices * time_devices, curves * frames_dev, share), jnp.bfloat16),
        spectra,
        mixers,
        *levels,
        mixers,
        place[: half * channels],
        centre,
        sums,
    )
    blocks = lax.all_to_all(blocks, ("chan", "tm"), split_axis=0, concat_axis=0, tiled=True)
    final = jnp.sum(blocks.astype(jnp.float32), axis=0)
    final = final * (1.0 / math.sqrt(length // 2))
    return jnp.transpose(final.reshape(curves, frames_dev, share), (2, 0, 1))


def solution(mesh):
    in_specs = (P(("groups", "chan", "beam"), "tm"), P(), P(), P(), P("chan", None))
    out_specs = P(("groups", "chan", "beam"), None, "tm")
    return jax.shard_map(shards, mesh=mesh, in_specs=in_specs, out_specs=out_specs, check_vma=False)
```
